32 devices in a mesh: row: 2 (over x), col: 16 (over z, y, core).
Axes of the slice: x: 2, y: 2, z: 4, core: 2. Of those that a mesh axis runs over, the one named last changes fastest.
Arguments:
- queries: bfloat16 [4096, 1024], P(('row', 'col')), may hold values from -24 to 24
- query_exps: int32 [4096], P(('row', 'col')), may hold values from -1 to 3
- key_head: bfloat16 [4096, 128], P(('col', 'row')), may hold values from -5 to 5
- value_head: bfloat16 [4096, 128], P(('col', 'row')), may hold values from -6 to 6
- forward_out: bfloat16 [4096, 1024], P(('row', 'col')), may hold values from -6 to 6
- output_grad: bfloat16 [4096, 1024], P(('row', 'col')), may hold values from -6 to 6
- stripe_order: int32 [32], replicated, may hold values from 0 to 31, each once
- window_size: int32 [1], replicated, may hold values from 1024 to 2048
Outputs:
- query_grad: bfloat16 [4096, 1024], P(('row', 'col'))
- key_grad: bfloat16 [4096, 128], P(('col', 'row'))
- value_grad: bfloat16 [4096, 128], P(('col', 'row'))
The draws below stay inside these ranges and needn't reach their ends.
Inputs may be any that keep to these rules, and one draw needn't show every extreme that they name: `stripe_order`: each stripe number appears once.
All inputs are finite; a program needn't handle non-finite values.
Results may differ from the reference program's by a relative error of at most 0.0095.
Values may be sent and summed in bfloat16 or wider, within the bound.
No kernel may reach another device: no remote copies, remote signals or barrier semaphores. Data moves between devices by JAX's collectives and lax.ppermute only.
A program may use at most 128 MiB of HBM per device.

```python
import math
import jax
import jax.numpy as jnp
from jax import lax

HEADS = 8
HEAD_DIM = 128
STRIPE = 128
TOK_DEV = 128
TOKENS = 4096
STRIPES = 32
WIN = 2048
N_ROW = 2


def base_keys(key):
    return jax.random.truncated_normal(jax.random.fold_in(key, 11), -4.0, 4.0, (TOKENS, HEAD_DIM), jnp.float32)


def draw_key_head(key, part):
    keys_drawn = base_keys(key)
    return keys_drawn.astype(jnp.bfloat16)


def draw_queries(key, part):
    result = jax.random.truncated_normal(jax.random.fold_in(key, 21), -4.0, 4.0, (TOKENS, HEADS * HEAD_DIM), jnp.float32)
    return result.astype(jnp.bfloat16)


def with_ends(drawn, stream_key, least, top_value):
    index_at = [jax.random.randint(jax.random.fold_in(stream_key, axis), (), 0, length) for axis, length in enumerate(drawn.shape)]
    main_axis = drawn.shape.index(max(drawn.shape))
    beside = index_at[:main_axis] + [(index_at[main_axis] + 1) % drawn.shape[main_axis]] + index_at[main_axis + 1:]
    return drawn.at[tuple(index_at)].set(least).at[tuple(beside)].set(top_value)


def shard_levels(rng, shape, pieces, low, high):
    def one(dim, parts):
        heights = jax.random.uniform(jax.random.fold_in(jax.random.fold_in(rng, 6), dim), (parts,), jnp.float32, low / len(pieces), high / len(pieces))
        return jnp.repeat(jnp.exp(heights), shape[dim] // parts).reshape((-1,) + (1,) * (len(shape) - dim - 1))

    level = one(*pieces[0])
    for cut in pieces[1:]:
        level = level * one(*cut)
    return level


def normal_values(own_key, extent, spread, reach, pieces=(), held_as=jnp.bfloat16):
    entries = jax.random.normal(own_key, extent, jnp.float32) * spread
    if len(pieces) > 0:
        entries = shard_levels(own_key, extent, pieces, -0.22, 0.18) * entries
    return jnp.clip(entries, min=-reach, max=reach).astype(held_as)


def setup_inputs(seed: int = 0) -> dict:
    arg_keys = jax.random.split(jax.random.key(seed), 9)
    return {
        "queries": draw_queries(jax.random.fold_in(arg_keys[8], 71), 0),
        "query_exps": with_ends(jax.random.randint(arg_keys[1], (TOKENS,), -1, 4), jax.random.fold_in(arg_keys[1], 1), -1, 3).astype(jnp.int32),
        "key_head": draw_key_head(jax.random.fold_in(arg_keys[8], 71), 0),
        "value_head": normal_values(arg_keys[3], (TOKENS, HEAD_DIM), 1.0, 6.0, ((0, 32),)),
        "forward_out": normal_values(arg_keys[4], (TOKENS, HEADS * HEAD_DIM), 1.0, 6.0, ((0, 32),)),
        "output_grad": normal_values(arg_keys[5], (TOKENS, HEADS * HEAD_DIM), 1.0, 6.0, ((0, 32),)),
        "stripe_order": jax.random.permutation(arg_keys[6], STRIPES).astype(jnp.int32),
        "window_size": jax.random.randint(arg_keys[7], (1,), WIN // 2, WIN + 1).astype(jnp.int32),
    }


neg_big = -1e+30

def reference(queries, query_exps, key_head, value_head, forward_out, output_grad, stripe_order, window_size):
    feat_width = HEADS * HEAD_DIM
    back_stripes = WIN // STRIPE
    span_stripes = back_stripes + 1
    inv_scale = 1.0 / math.sqrt(HEAD_DIM)
    window_len = window_size[0]
    highest_prec = lax.Precision.HIGHEST
    scaled = (queries.astype(jnp.float32) * jnp.exp2(query_exps.astype(jnp.float32))[:, None]).astype(jnp.bfloat16)
    product = output_grad.astype(jnp.float32) * forward_out.astype(jnp.float32)
    head_delta = product.reshape(TOKENS, HEADS, HEAD_DIM).sum(-1).astype(jnp.bfloat16)
    inverse = jnp.zeros((STRIPES,), jnp.int32).at[stripe_order].set(jnp.arange(STRIPES, dtype=jnp.int32))

    def by_position(array):
        blocks = array.reshape((STRIPES, STRIPE) + array.shape[1:])
        return blocks[inverse]
    q_pos = by_position(scaled)
    g_pos = by_position(output_grad)
    d_pos = by_position(head_delta)
    padding = ((back_stripes, 0), (0, 0), (0, 0))
    k_pad = jnp.pad(by_position(key_head), padding).reshape(-1, HEAD_DIM)
    v_pad = jnp.pad(by_position(value_head), padding).reshape(-1, HEAD_DIM)
    key_panel = inverse * STRIPE // TOK_DEV % N_ROW
    owner_pad = jnp.pad(key_panel, (back_stripes, 0))
    offsets = jnp.arange(STRIPE, dtype=jnp.int32)
    key_offsets = jnp.arange(span_stripes * STRIPE, dtype=jnp.int32)
    panels = jnp.arange(N_ROW, dtype=jnp.int32)

    def one_stripe(carried, stripe_id):
        dk_acc, dv_acc = carried
        row_start = stripe_id * STRIPE
        query_tile = q_pos[stripe_id].astype(jnp.float32).reshape(STRIPE, HEADS, HEAD_DIM)
        grad_tile = g_pos[stripe_id].astype(jnp.float32).reshape(STRIPE, HEADS, HEAD_DIM)
        delta_tile = d_pos[stripe_id].astype(jnp.float32)
        key_rows = lax.dynamic_slice_in_dim(k_pad, row_start, span_stripes * STRIPE).astype(jnp.float32)
        value_rows = lax.dynamic_slice_in_dim(v_pad, row_start, span_stripes * STRIPE).astype(jnp.float32)
        owners = lax.dynamic_slice_in_dim(owner_pad, stripe_id, span_stripes)
        query_at = row_start + offsets
        key_at = row_start - back_stripes * STRIPE + key_offsets
        distance = query_at[:, None] - key_at[None, :]
        visible = ((distance >= 0) & (distance < window_len) & (key_at[None, :] >= 0))[None]
        scores = jnp.einsum('ihd,jd->hij', query_tile, key_rows, precision=highest_prec) * inv_scale
        highest = lax.optimization_barrier(jnp.max(jnp.where(visible, scores, neg_big), axis=2, keepdims=True))
        normaliser = lax.optimization_barrier(jnp.sum(jnp.exp(jnp.where(visible, scores - highest, neg_big)), axis=2, keepdims=True))
        log_norm = highest + jnp.log(normaliser)
        weights = jnp.exp(jnp.where(visible, scores - log_norm, neg_big))
        rounded_weights = lax.optimization_barrier(weights.astype(jnp.bfloat16)).astype(jnp.float32)
        weight_grad = jnp.einsum('ihd,jd->hij', grad_tile, value_rows, precision=highest_prec)
        score_grad = (weights * (weight_grad - delta_tile.T[:, :, None])).astype(jnp.bfloat16)
        score_grad = lax.optimization_barrier(score_grad).astype(jnp.float32)
        dq_parts = jnp.einsum('hinj,njd->nihd', score_grad.reshape(HEADS, STRIPE, span_stripes, STRIPE), key_rows.reshape(span_stripes, STRIPE, HEAD_DIM), precision=highest_prec) * inv_scale
        onehot = (owners[:, None] == panels[None, :]).astype(jnp.float32)
        partial_value = jnp.einsum('nc,nihd->cihd', onehot, dq_parts, precision=highest_prec)
        partial_value = lax.optimization_barrier(partial_value.astype(jnp.bfloat16)).astype(jnp.float32)
        query_part = partial_value.sum(0).reshape(STRIPE, feat_width).astype(jnp.bfloat16)
        key_part = jnp.einsum('hij,ihd->jd', score_grad, query_tile, precision=highest_prec) * inv_scale
        value_part = jnp.einsum('hij,ihd->jd', rounded_weights, grad_tile, precision=highest_prec)
        old_keys = lax.dynamic_slice_in_dim(dk_acc, row_start, span_stripes * STRIPE)
        old_values = lax.dynamic_slice_in_dim(dv_acc, row_start, span_stripes * STRIPE)
        dk_acc = lax.dynamic_update_slice_in_dim(dk_acc, old_keys + key_part, row_start, 0)
        dv_acc = lax.dynamic_update_slice_in_dim(dv_acc, old_values + value_part, row_start, 0)
        return ((dk_acc, dv_acc), query_part)
    zero_rows = jnp.zeros(((STRIPES + back_stripes) * STRIPE, HEAD_DIM), jnp.float32)
    (dk_acc, dv_acc), query_stack = lax.scan(one_stripe, (zero_rows, zero_rows), jnp.arange(STRIPES, dtype=jnp.int32))
    dk_stack = dk_acc[back_stripes * STRIPE:].reshape(STRIPES, STRIPE, HEAD_DIM)
    dv_stack = dv_acc[back_stripes * STRIPE:].reshape(STRIPES, STRIPE, HEAD_DIM)
    query_grad = query_stack[stripe_order].reshape(TOKENS, feat_width)
    key_grad = dk_stack[stripe_order].reshape(TOKENS, HEAD_DIM).astype(jnp.bfloat16)
    value_grad = dv_stack[stripe_order].reshape(TOKENS, HEAD_DIM).astype(jnp.bfloat16)
    return (query_grad, key_grad, value_grad)
```

```python
import functools
import math

import jax
import jax.numpy as jnp
from jax import lax
from jax.experimental import pallas as pl
from jax.experimental.pallas import tpu as pltpu
from jax.sharding import PartitionSpec as P

STRIPE = 128
AXES = ("row", "col")
neg_big = -1e30
far_away = 1 << 29
keep_bytes = 24 << 20


class Layout:
    def __init__(self, rows, cols):
        self.rows, self.cols = rows, cols
        self.near, self.far = rows * 2, cols // 4
        self.square = self.near == self.far
        self.count = rows * cols

    def split(self, row, col):
        return row * 2 + (col // 2) % 2, col // 4, col % 2

    def join(self, near, far, core):
        return (near // 2) * self.cols + far * 4 + (near % 2) * 2 + core

    def hop(self, first=0, second=0, core_flip=0):
        pairs = []
        for device in range(self.count):
            near, far, core = self.split(device // self.cols, device % self.cols)
            if self.square and core == 1:
                near, far = near ^ second, far ^ first
            else:
                near, far = near ^ first, far ^ second
            pairs.append((device, self.join(near, far, core ^ core_flip)))
        return pairs

    def slot(self, own, other, core):
        near, far, its_core = own[0] ^ other[0], own[1] ^ other[1], core ^ other[2]
        plain = far * (2 * self.near) + near * 2 + its_core
        if not self.square:
            return plain
        turned = near * (2 * self.far) + far * 2 + its_core
        return jnp.where(core == 1, turned, plain)


def dot(left, right, left_dim, right_dim):
    return lax.dot_general(
        left, right, (((left_dim,), (right_dim,)), ((), ())), preferred_element_type=jnp.float32
    )


def attend(
    stripes, pieces, heads, keep, inv_scale,
    meta, q_ref, g_ref, delta_ref, *refs,
):
    held, rest = refs[: 2 * pieces], refs[2 * pieces :]
    dq_ref, sent, rest = rest[0], rest[1 : 1 + 2 * pieces], rest[1 + 2 * pieces :]
    kv, grads, probs, tops, weight_buf, grad_buf, run_max, run_sum, in_sem, out_sem = rest
    piece_rows = stripes // pieces * STRIPE
    to_log2 = inv_scale * math.log2(math.e)
    live, window_len = meta[0], meta[1]
    turns = (live + 1) // 2
    k_at, v_at = 2, 2 + stripes + 2

    copies = [
        pltpu.make_async_copy(ref, kv.at[pl.ds(i * piece_rows, piece_rows)], in_sem.at[i])
        for i, ref in enumerate(held)
    ]
    for copy in copies:
        copy.start()
    grads[...] = jnp.zeros_like(grads)
    kv[pl.ds(2 * stripes * STRIPE, STRIPE)] = jnp.zeros((STRIPE, STRIPE), kv.dtype)
    run_max[...] = jnp.full_like(run_max, neg_big)
    run_sum[...] = jnp.zeros_like(run_sum)
    dq_ref[...] = jnp.zeros_like(dq_ref)
    for copy in copies:
        copy.wait()

    relative = lax.broadcasted_iota(jnp.int32, (STRIPE, STRIPE), 1) - lax.broadcasted_iota(
        jnp.int32, (STRIPE, STRIPE), 0
    )

    def rows_of(start, turn):
        offsets = [pl.multiple_of(meta[start + 2 * turn + i], STRIPE) for i in range(2)]
        return offsets, jnp.concatenate([kv[pl.ds(offset, STRIPE)] for offset in offsets], 0)

    def visible_at(turn):
        masks = []
        for i in range(2):
            block = 2 * turn + i
            distance = relative + jnp.where(block < live, block * STRIPE, far_away)
            masks.append((distance >= 0) & (distance < window_len))
        return jnp.concatenate(masks, 0)

    def head_cols(head):
        return pl.ds(head * STRIPE, STRIPE)

    def masked_scores(key_rows, visible, head):
        scores = dot(key_rows, q_ref[head_cols(head)], 1, 1) * to_log2
        return jnp.where(visible, scores, neg_big)

    def add_stats(turn, carry):
        _, key_rows = rows_of(k_at, turn)
        visible = visible_at(turn)
        for head in range(heads):
            cols = head_cols(head)
            scores = masked_scores(key_rows, visible, head)
            old_max = run_max[:, cols]
            new_max = jnp.maximum(old_max, jnp.max(scores, axis=0, keepdims=True))
            part = jnp.exp2(scores - new_max)
            summed = jnp.sum(part.reshape(-1, 8, STRIPE), axis=0)
            run_sum[:, cols] = run_sum[:, cols] * jnp.exp2(old_max - new_max) + summed
            run_max[:, cols] = new_max
            if keep:
                probs[turn, :, cols] = part
                tops[turn, :, cols] = new_max
        return carry

    lax.fori_loop(0, turns, add_stats, 0)
    total = jnp.sum(run_sum[...], axis=0, keepdims=True)
    inverse = 1.0 / total
    run_sum[pl.ds(0, 1)] = inverse

    def add_grads(turn, carry):
        key_offsets, key_rows = rows_of(k_at, turn)
        value_offsets, value_rows = rows_of(v_at, turn)
        if not keep:
            visible = visible_at(turn)
        for head in range(heads):
            cols = head_cols(head)
            if keep:
                factor = jnp.exp2(tops[turn, :, cols] - run_max[:, cols]) * run_sum[pl.ds(0, 1), cols]
                weights = probs[turn, :, cols] * factor
            else:
                scores = masked_scores(key_rows, visible, head)
                weights = jnp.exp2(scores - run_max[:, cols]) * run_sum[pl.ds(0, 1), cols]
            weight_grad = dot(value_rows, g_ref[cols], 1, 1)
            score_grad = weights * (weight_grad - delta_ref[:, cols])
            weight_buf[:, cols] = weights.astype(jnp.bfloat16)
            grad_buf[:, cols] = score_grad.astype(jnp.bfloat16)
        score_grads = grad_buf[...]
        dq_ref[...] += dot(key_rows, score_grads, 0, 0)
        key_part = (dot(score_grads, q_ref[...], 1, 0) * inv_scale).astype(jnp.bfloat16)
        value_part = dot(weight_buf[...], g_ref[...], 1, 0).astype(jnp.bfloat16)
        for i in range(2):
            grads[pl.ds(key_offsets[i], STRIPE)] = key_part[i * STRIPE : (i + 1) * STRIPE]
            grads[pl.ds(value_offsets[i], STRIPE)] = value_part[i * STRIPE : (i + 1) * STRIPE]
        return carry

    lax.fori_loop(0, turns, add_grads, 0)
    copies = [
        pltpu.make_async_copy(grads.at[pl.ds(i * piece_rows, piece_rows)], ref, out_sem.at[i])
        for i, ref in enumerate(sent)
    ]
    for copy in copies:
        copy.start()
    for copy in copies:
        copy.wait()


def run_attend(meta, q_flat, g_flat, delta, held, stripes, heads, inv_scale):
    pieces = len(held) // 2
    wide = q_flat.shape[0]
    turns = stripes // 2 + 1
    keep = turns * 2 * STRIPE * wide * 4 <= keep_bytes
    kept = turns if keep else 1
    rows = (2 * stripes + 1) * STRIPE
    any_spec = pl.BlockSpec(memory_space=pl.ANY)
    vmem_spec = pl.BlockSpec(memory_space=pltpu.VMEM)
    return pl.pallas_call(
        functools.partial(attend, stripes, pieces, heads, keep, inv_scale),
        out_shape=[jax.ShapeDtypeStruct((STRIPE, wide), jnp.float32)]
        + [jax.ShapeDtypeStruct(piece.shape, piece.dtype) for piece in held],
        in_specs=[pl.BlockSpec(memory_space=pltpu.SMEM)] + [vmem_spec] * 3 + [any_spec] * len(held),
        out_specs=[vmem_spec] + [any_spec] * len(held),
        scratch_shapes=[
            pltpu.VMEM((rows, STRIPE), jnp.bfloat16),
            pltpu.VMEM((rows, STRIPE), jnp.bfloat16),
            pltpu.VMEM((kept, 2 * STRIPE, wide), jnp.float32),
            pltpu.VMEM((kept, 1, wide), jnp.float32),
            pltpu.VMEM((2 * STRIPE, wide), jnp.bfloat16),
            pltpu.VMEM((2 * STRIPE, wide), jnp.bfloat16),
            pltpu.VMEM((1, wide), jnp.float32),
            pltpu.VMEM((8, wide), jnp.float32),
            pltpu.SemaphoreType.DMA((len(held),)),
            pltpu.SemaphoreType.DMA((len(held),)),
        ],
        name="attend",
    )(meta, q_flat, g_flat, delta, *held)


def visit_table(layout, stripe_order, window_len, row, col):
    stripes = layout.count
    own = layout.split(row, col)
    core = own[2]
    stored = jnp.arange(stripes, dtype=jnp.int32)
    other = layout.split(stored % layout.rows, stored // layout.rows)
    mine = layout.slot(own, other, core)
    theirs = layout.slot(own, other, 1 - core) + stripes
    key_slot = jnp.where(core == 0, mine, theirs)
    value_slot = jnp.where(core == 0, theirs, mine)
    own_block = jnp.sum(jnp.where(stored == row * layout.cols + col, stripe_order, 0))
    live = jnp.minimum(own_block, (window_len + STRIPE - 2) // STRIPE) + 1
    back = jnp.arange(stripes + 2, dtype=jnp.int32)
    match = (stripe_order[None, :] == own_block - back[:, None]) & (back[:, None] < live)
    spare = 2 * stripes
    key_at = spare + jnp.sum(jnp.where(match, key_slot[None, :] - spare, 0), axis=1)
    value_at = spare + jnp.sum(jnp.where(match, value_slot[None, :] - spare, 0), axis=1)
    head = jnp.stack([live, window_len])
    return jnp.concatenate([head, key_at * STRIPE, value_at * STRIPE]).astype(jnp.int32)


def per_device(
    layout,
    queries, query_exps, key_head, value_head, forward_out, output_grad, stripe_order, window_size
):
    head_dim = key_head.shape[1]
    tokens, feat_width = queries.shape
    heads = feat_width // head_dim
    inv_scale = 1.0 / math.sqrt(head_dim)
    stripes = layout.count
    row, col = lax.axis_index("row"), lax.axis_index("col")
    core = col % 2
    second_size = layout.far
    first_size = layout.near

    def send(value, **where):
        return lax.ppermute(value, AXES, layout.hop(**where))

    first_core = core == 0
    kept = jnp.where(first_core, key_head, value_head)
    given = jnp.where(first_core, value_head, key_head)
    pair = jnp.concatenate([kept, send(given, core_flip=1)], 0)
    plane = jnp.concatenate([pair] + [send(pair, first=i) for i in range(1, first_size)], 0)
    own_pieces = [plane] + [send(plane, second=j) for j in range(1, second_size)]
    other_pieces = [send(piece, core_flip=1) for piece in own_pieces]

    def by_head(value):
        return value.reshape(tokens, heads, head_dim).transpose(1, 0, 2).reshape(-1, head_dim)

    power = jnp.left_shift(1, query_exps + 1).astype(jnp.float32) * 0.5
    scaled = (queries.astype(jnp.float32) * power[:, None]).astype(jnp.bfloat16)
    product = output_grad.astype(jnp.float32) * forward_out.astype(jnp.float32)
    delta = product.reshape(tokens, heads, head_dim).sum(-1).astype(jnp.bfloat16)
    delta_row = delta.astype(jnp.float32).T.reshape(1, -1)
    meta = visit_table(layout, stripe_order, window_size[0], row, col)
    results = run_attend(
        meta, by_head(scaled), by_head(output_grad), delta_row,
        own_pieces + other_pieces, stripes, heads, inv_scale,
    )
    query_turned, own_parts, other_parts = (
        results[0], results[1 : 1 + second_size], results[1 + second_size :]
    )

    def widen(value):
        return value.astype(jnp.float32)

    summed = [
        widen(own) + widen(send(other, core_flip=1)) for own, other in zip(own_parts, other_parts)
    ]
    plane_sum = summed[0]
    for j in range(1, second_size):
        plane_sum = plane_sum + widen(send(summed[j].astype(jnp.bfloat16), second=j))
    pair_rows = 2 * tokens
    pair_sum = plane_sum[:pair_rows]
    for i in range(1, first_size):
        part = plane_sum[i * pair_rows : (i + 1) * pair_rows].astype(jnp.bfloat16)
        pair_sum = pair_sum + widen(send(part, first=i))
    pair_sum = pair_sum.astype(jnp.bfloat16)
    own_grad, given_grad = pair_sum[:tokens], send(pair_sum[tokens:], core_flip=1)
    key_grad = jnp.where(first_core, own_grad, given_grad)
    value_grad = jnp.where(first_core, given_grad, own_grad)
    query_grad = (query_turned * inv_scale).astype(jnp.bfloat16)
    query_grad = query_grad.reshape(head_dim, heads, tokens).transpose(2, 1, 0)
    return (query_grad.reshape(tokens, feat_width), key_grad, value_grad)


def solution(mesh):
    layout = Layout(mesh.shape["row"], mesh.shape["col"])
    return jax.shard_map(
        functools.partial(per_device, layout),
        mesh=mesh,
        in_specs=(
            P(("row", "col"), None),
            P(("row", "col")),
            P(("col", "row"), None),
            P(("col", "row"), None),
            P(("row", "col"), None),
            P(("row", "col"), None),
            P(),
            P(),
        ),
        out_specs=(P(("row", "col"), None), P(("col", "row"), None), P(("col", "row"), None)),
        check_vma=False,
    )
```

```python
import functools
import math

import jax
import jax.numpy as jnp
from jax import lax
from jax.experimental import pallas as pl
from jax.experimental.pallas import tpu as pltpu
from jax.sharding import PartitionSpec as P

STRIPE = 128
PAIR = 2 * STRIPE
AXES = ("row", "col")
neg_big = -1e30
far_away = 1 << 29
keep_bytes = 24 << 20


class Layout:
    def __init__(self, rows, cols):
        self.rows, self.cols = rows, cols
        self.near, self.far = rows * 2, cols // 4
        self.square = self.near == self.far
        self.count = rows * cols

    def split(self, row, col):
        return row * 2 + (col // 2) % 2, col // 4, col % 2

    def join(self, near, far, core):
        return (near // 2) * self.cols + far * 4 + (near % 2) * 2 + core

    def hop(self, first=0, second=0, core_flip=0):
        pairs = []
        for device in range(self.count):
            near, far, core = self.split(device // self.cols, device % self.cols)
            if self.square and core == 1:
                near, far = near ^ second, far ^ first
            else:
                near, far = near ^ first, far ^ second
            pairs.append((device, self.join(near, far, core ^ core_flip)))
        return pairs

    def slot(self, own, stored):
        near, far, core = self.split(stored % self.rows, stored // self.rows)
        near, far = near ^ own[0], far ^ own[1]
        place = far * self.near + near
        if self.square:
            place = jnp.where(core == 1, near * self.far + far, place)
        return place + jnp.where(core == own[2], 0, self.count // 2)


def dot(left, right, left_dim, right_dim):
    return lax.dot_general(
        left, right, (((left_dim,), (right_dim,)), ((), ())), preferred_element_type=jnp.float32
    )


def prepare(layout, heads, here, order, window, q_ref, e_ref, g_ref, o_ref, q_out, g_out, d_out, meta):
    row, col = here[0], here[1]
    own = layout.split(row, col)
    own_block = order[row * layout.cols + col]
    live = jnp.minimum(own_block, (window[0] + STRIPE - 2) // STRIPE) + 1
    meta[0] = live
    meta[1] = window[0]

    def clear(back, carry):
        meta[2 + back] = layout.count * PAIR
        return carry

    def place(stored, carry):
        back = own_block - order[stored]

        @pl.when((back >= 0) & (back < live))
        def _():
            meta[2 + back] = layout.slot(own, stored) * PAIR

        return carry

    lax.fori_loop(0, layout.count + 2, clear, 0)
    lax.fori_loop(0, layout.count, place, 0)
    power = jnp.left_shift(1, e_ref[...] + 1).astype(jnp.float32) * 0.5
    power = jnp.broadcast_to(power, (STRIPE, STRIPE)).T
    for head in range(heads):
        cols = pl.ds(head * STRIPE, STRIPE)
        q_out[cols] = (q_ref[:, cols].astype(jnp.float32) * power).astype(jnp.bfloat16)
        grads = g_ref[:, cols]
        g_out[cols] = grads
        product = grads.astype(jnp.float32) * o_ref[:, cols].astype(jnp.float32)
        sums = jnp.sum(product.T, axis=0, keepdims=True)
        d_out[:, cols] = sums.astype(jnp.bfloat16).astype(jnp.float32)


def attend(
    stripes, pieces, heads, keep, inv_scale,
    meta, q_ref, g_ref, delta_ref, *refs,
):
    held, rest = refs[: 2 * pieces], refs[2 * pieces :]
    dq_ref, own_out, other_out, rest = rest[0], rest[1], rest[2 : 2 + pieces], rest[2 + pieces :]
    kv, probs, tops, weight_buf, grad_buf, run_max, run_sum = rest
    half_rows = stripes // 2 * PAIR
    piece_rows = half_rows // pieces
    to_log2 = inv_scale * math.log2(math.e)
    live, window_len = meta[0], meta[1]
    turns = (live + 1) // 2

    for i, ref in enumerate(held):
        kv[pl.ds(i * piece_rows, piece_rows)] = ref[...]
    kv[pl.ds(2 * half_rows, PAIR)] = jnp.zeros((PAIR, STRIPE), kv.dtype)
    for ref in (own_out, *other_out):
        ref[...] = jnp.zeros_like(ref)
    run_max[...] = jnp.full_like(run_max, neg_big)
    run_sum[...] = jnp.zeros_like(run_sum)
    dq_ref[...] = jnp.zeros_like(dq_ref)

    relative = lax.broadcasted_iota(jnp.int32, (STRIPE, STRIPE), 1) - lax.broadcasted_iota(
        jnp.int32, (STRIPE, STRIPE), 0
    )

    def offsets_of(turn):
        return [pl.multiple_of(meta[2 + 2 * turn + i], PAIR) for i in range(2)]

    def rows_at(offsets, shift):
        return jnp.concatenate([kv[pl.ds(offset + shift, STRIPE)] for offset in offsets], 0)

    def visible_at(turn):
        masks = []
        for i in range(2):
            block = 2 * turn + i
            distance = relative + jnp.where(block < live, block * STRIPE, far_away)
            masks.append((distance >= 0) & (distance < window_len))
        return jnp.concatenate(masks, 0)

    def head_cols(head):
        return pl.ds(head * STRIPE, STRIPE)

    def masked_scores(key_rows, visible, head):
        scores = dot(key_rows, q_ref[head_cols(head)], 1, 1) * to_log2
        return jnp.where(visible, scores, neg_big)

    def add_stats(turn, carry):
        key_rows = rows_at(offsets_of(turn), 0)
        visible = visible_at(turn)
        for head in range(heads):
            cols = head_cols(head)
            scores = masked_scores(key_rows, visible, head)
            old_max = run_max[:, cols]
            new_max = jnp.maximum(old_max, jnp.max(scores, axis=0, keepdims=True))
            part = jnp.exp2(scores - new_max)
            summed = jnp.sum(part.reshape(-1, 8, STRIPE), axis=0)
            run_sum[:, cols] = run_sum[:, cols] * jnp.exp2(old_max - new_max) + summed
            run_max[:, cols] = new_max
            if keep:
                probs[turn, :, cols] = part
                tops[turn, :, cols] = new_max
        return carry

    lax.fori_loop(0, turns, add_stats, 0)
    total = jnp.sum(run_sum[...], axis=0, keepdims=True)
    run_sum[pl.ds(0, 1)] = 1.0 / total

    def add_grads(turn, carry):
        offsets = offsets_of(turn)
        key_rows, value_rows = rows_at(offsets, 0), rows_at(offsets, STRIPE)
        if not keep:
            visible = visible_at(turn)
        for head in range(heads):
            cols = head_cols(head)
            if keep:
                factor = jnp.exp2(tops[turn, :, cols] - run_max[:, cols]) * run_sum[pl.ds(0, 1), cols]
                weights = probs[turn, :, cols] * factor
            else:
                scores = masked_scores(key_rows, visible, head)
                weights = jnp.exp2(scores - run_max[:, cols]) * run_sum[pl.ds(0, 1), cols]
            weight_grad = dot(value_rows, g_ref[cols], 1, 1)
            score_grad = weights * (weight_grad - delta_ref[:, cols])
            weight_buf[:, cols] = weights.astype(jnp.bfloat16)
            grad_buf[:, cols] = score_grad.astype(jnp.bfloat16)
        score_grads = grad_buf[...]
        dq_ref[...] += dot(key_rows, score_grads, 0, 0)
        key_part = (dot(score_grads, q_ref[...], 1, 0) * inv_scale).astype(jnp.bfloat16)
        value_part = dot(weight_buf[...], g_ref[...], 1, 0).astype(jnp.bfloat16)
        for i, offset in enumerate(offsets):
            part = slice(i * STRIPE, (i + 1) * STRIPE)
            spans = [(0, half_rows, own_out)] + [
                (half_rows + j * piece_rows, piece_rows, ref) for j, ref in enumerate(other_out)
            ]
            for start, length, ref in spans:

                @pl.when((offset >= start) & (offset < start + length))
                def _(start=start, ref=ref):
                    inner = pl.multiple_of(offset - start, PAIR)
                    ref[pl.ds(inner, STRIPE)] = key_part[part]
                    ref[pl.ds(inner + STRIPE, STRIPE)] = value_part[part]

        return carry

    lax.fori_loop(0, turns, add_grads, 0)


def turn_queries(heads, inv_scale, turned, out):
    for head in range(heads):
        cols = pl.ds(head * STRIPE, STRIPE)
        out[:, cols] = (turned[:, cols].T * inv_scale).astype(jnp.bfloat16)


vmem_spec = pl.BlockSpec(memory_space=pltpu.VMEM)
smem_spec = pl.BlockSpec(memory_space=pltpu.SMEM)


def run_prepare(layout, heads, here, order, window, queries, exps, grads, outs):
    flat = jax.ShapeDtypeStruct((heads * STRIPE, STRIPE), jnp.bfloat16)
    return pl.pallas_call(
        functools.partial(prepare, layout, heads),
        out_shape=[
            flat,
            flat,
            jax.ShapeDtypeStruct((1, heads * STRIPE), jnp.float32),
            jax.ShapeDtypeStruct((layout.count + 4,), jnp.int32),
        ],
        in_specs=[smem_spec] * 3 + [vmem_spec] * 4,
        out_specs=[vmem_spec] * 3 + [smem_spec],
        name="prep",
    )(here, order, window, queries, exps, grads, outs)


def run_attend(meta, q_flat, g_flat, delta, held, stripes, heads, inv_scale):
    pieces = len(held) // 2
    wide = q_flat.shape[0]
    turns = stripes // 2 + 1
    keep = turns * PAIR * wide * 4 <= keep_bytes
    kept = turns if keep else 1
    half_rows = stripes // 2 * PAIR
    other = jax.ShapeDtypeStruct((half_rows // pieces, STRIPE), jnp.bfloat16)
    return pl.pallas_call(
        functools.partial(attend, stripes, pieces, heads, keep, inv_scale),
        out_shape=[
            jax.ShapeDtypeStruct((STRIPE, wide), jnp.float32),
            jax.ShapeDtypeStruct((half_rows, STRIPE), jnp.bfloat16),
        ]
        + [other] * pieces,
        in_specs=[smem_spec] + [vmem_spec] * (3 + len(held)),
        out_specs=[vmem_spec] * (2 + pieces),
        scratch_shapes=[
            pltpu.VMEM((2 * half_rows + PAIR, STRIPE), jnp.bfloat16),
            pltpu.VMEM((kept, PAIR, wide), jnp.float32),
            pltpu.VMEM((kept, 1, wide), jnp.float32),
            pltpu.VMEM((PAIR, wide), jnp.bfloat16),
            pltpu.VMEM((PAIR, wide), jnp.bfloat16),
            pltpu.VMEM((1, wide), jnp.float32),
            pltpu.VMEM((8, wide), jnp.float32),
        ],
        name="attend",
    )(meta, q_flat, g_flat, delta, *held)


def run_turn(turned, heads, inv_scale):
    return pl.pallas_call(
        functools.partial(turn_queries, heads, inv_scale),
        out_shape=jax.ShapeDtypeStruct(turned.shape, jnp.bfloat16),
        in_specs=[vmem_spec],
        out_specs=vmem_spec,
        name="turn",
    )(turned)


def per_device(
    layout,
    queries, query_exps, key_head, value_head, forward_out, output_grad, stripe_order, window_size
):
    head_dim = key_head.shape[1]
    tokens, feat_width = queries.shape
    heads = feat_width // head_dim
    inv_scale = 1.0 / math.sqrt(head_dim)
    stripes = layout.count
    row, col = lax.axis_index("row"), lax.axis_index("col")

    def send(value, **where):
        return lax.ppermute(value, AXES, layout.hop(**where))

    def widen(value):
        return value.astype(jnp.float32)

    pair = jnp.concatenate([key_head, value_head], 0)
    stage = [pair] + [send(pair, first=i) for i in range(1, layout.near)]
    plane = jnp.concatenate(stage, 0)
    own_pieces = [plane] + [send(plane, second=j) for j in range(1, layout.far)]
    other_pieces = [send(piece, core_flip=1) for piece in own_pieces]

    here = jnp.stack([row, col]).astype(jnp.int32)
    q_flat, g_flat, delta, meta = run_prepare(
        layout, heads, here, stripe_order, window_size,
        queries, query_exps.reshape(1, -1), output_grad, forward_out,
    )
    results = run_attend(
        meta, q_flat, g_flat, delta, own_pieces + other_pieces, stripes, heads, inv_scale
    )
    turned, own_part, other_parts = results[0], results[1], results[2:]
    query_grad = run_turn(turned, heads, inv_scale)

    piece_rows = plane.shape[0]
    summed = [
        widen(own_part[j * piece_rows : (j + 1) * piece_rows])
        + widen(send(other_parts[j], core_flip=1))
        for j in range(layout.far)
    ]
    plane_sum = summed[0]
    for j in range(1, layout.far):
        plane_sum = plane_sum + widen(send(summed[j].astype(jnp.bfloat16), second=j))
    pair_sum = plane_sum[:PAIR]
    for i in range(1, layout.near):
        part = plane_sum[i * PAIR : (i + 1) * PAIR].astype(jnp.bfloat16)
        pair_sum = pair_sum + widen(send(part, first=i))
    pair_sum = pair_sum.astype(jnp.bfloat16)
    return (query_grad, pair_sum[:tokens], pair_sum[tokens:])


def solution(mesh):
    layout = Layout(mesh.shape["row"], mesh.shape["col"])

    def whole(*arrays):
        return per_device(layout, *arrays)

    return jax.shard_map(
        whole,
        mesh=mesh,
        in_specs=(
            P(("row", "col"), None),
            P(("row", "col")),
            P(("col", "row"), None),
            P(("col", "row"), None),
            P(("row", "col"), None),
            P(("row", "col"), None),
            P(),
            P(),
        ),
        out_specs=(P(("row", "col"), None), P(("col", "row"), None), P(("col", "row"), None)),
        check_vma=False,
    )
```

```python
import functools
import math

import jax
import jax.numpy as jnp
from jax import lax
from jax.experimental import pallas as pl
from jax.experimental.pallas import tpu as pltpu
from jax.sharding import PartitionSpec as P

STRIPE = 128
PAIR = 2 * STRIPE
AXES = ("row", "col")
neg_big = -1e30
far_away = 1 << 29
keep_bytes = 24 << 20


class Layout:
    def __init__(self, rows, cols):
        self.rows, self.cols = rows, cols
        self.near, self.far = rows * 2, cols // 4
        self.square = self.near == self.far
        self.count = rows * cols

    def split(self, row, col):
        ring = col // 4
        half = ring // 2
        return row * 2 + (ring + half) % 2, half * 2 + (col // 2) % 2, col % 2

    def join(self, near, far, core):
        half = far // 2
        ring = half * 2 + (near + half) % 2
        return (near // 2) * self.cols + ring * 4 + (far % 2) * 2 + core

    def hop(self, first=0, second=0, core_flip=0):
        pairs = []
        for device in range(self.count):
            near, far, core = self.split(device // self.cols, device % self.cols)
            if self.square and core == 1:
                near, far = near ^ second, far ^ first
            else:
                near, far = near ^ first, far ^ second
            pairs.append((device, self.join(near, far, core ^ core_flip)))
        return pairs

    def slot(self, own, stored):
        near, far, core = self.split(stored % self.rows, stored // self.rows)
        near, far = near ^ own[0], far ^ own[1]
        place = far * self.near + near
        if self.square:
            place = jnp.where(core == 1, near * self.far + far, place)
        return place + jnp.where(core == own[2], 0, self.count // 2)


def dot(left, right, left_dim, right_dim):
    return lax.dot_general(
        left, right, (((left_dim,), (right_dim,)), ((), ())), preferred_element_type=jnp.float32
    )


def prepare(layout, heads, here, order, window, q_ref, e_ref, g_ref, o_ref, q_out, g_out, d_out, meta):
    row, col = here[0], here[1]
    own = layout.split(row, col)
    own_block = order[row * layout.cols + col]
    live = jnp.minimum(own_block, (window[0] + STRIPE - 2) // STRIPE) + 1
    meta[0] = live
    meta[1] = window[0]

    def clear(back, carry):
        meta[2 + back] = layout.count * PAIR
        return carry

    def place(stored, carry):
        back = own_block - order[stored]

        @pl.when((back >= 0) & (back < live))
        def _():
            meta[2 + back] = layout.slot(own, stored) * PAIR

        return carry

    lax.fori_loop(0, layout.count + 2, clear, 0)
    lax.fori_loop(0, layout.count, place, 0)
    power = jnp.left_shift(1, e_ref[...] + 1).astype(jnp.float32) * 0.5
    power = jnp.broadcast_to(power, (STRIPE, STRIPE)).T
    for head in range(heads):
        cols = pl.ds(head * STRIPE, STRIPE)
        q_out[cols] = (q_ref[:, cols].astype(jnp.float32) * power).astype(jnp.bfloat16)
        grads = g_ref[:, cols]
        g_out[cols] = grads
        product = grads.astype(jnp.float32) * o_ref[:, cols].astype(jnp.float32)
        sums = jnp.sum(product.T, axis=0, keepdims=True)
        d_out[:, cols] = sums.astype(jnp.bfloat16).astype(jnp.float32)


def attend(
    stripes, pieces, heads, keep, inv_scale,
    meta, q_ref, g_ref, delta_ref, *refs,
):
    held, rest = refs[: 2 * pieces], refs[2 * pieces :]
    dq_ref, own_out, other_out, rest = rest[0], rest[1], rest[2 : 2 + pieces], rest[2 + pieces :]
    kv, probs, tops, weight_buf, grad_buf, run_max, run_sum = rest
    half_rows = stripes // 2 * PAIR
    piece_rows = half_rows // pieces
    to_log2 = inv_scale * math.log2(math.e)
    live, window_len = meta[0], meta[1]
    turns = (live + 1) // 2

    for i, ref in enumerate(held):
        kv[pl.ds(i * piece_rows, piece_rows)] = ref[...]
    kv[pl.ds(2 * half_rows, PAIR)] = jnp.zeros((PAIR, STRIPE), kv.dtype)
    for ref in (own_out, *other_out):
        ref[...] = jnp.zeros_like(ref)
    run_max[...] = jnp.full_like(run_max, neg_big)
    run_sum[...] = jnp.zeros_like(run_sum)
    dq_ref[...] = jnp.zeros_like(dq_ref)

    relative = lax.broadcasted_iota(jnp.int32, (STRIPE, STRIPE), 1) - lax.broadcasted_iota(
        jnp.int32, (STRIPE, STRIPE), 0
    )

    def offsets_of(turn):
        return [pl.multiple_of(meta[2 + 2 * turn + i], PAIR) for i in range(2)]

    def rows_at(offsets, shift):
        return jnp.concatenate([kv[pl.ds(offset + shift, STRIPE)] for offset in offsets], 0)

    def visible_at(turn):
        masks = []
        for i in range(2):
            block = 2 * turn + i
            distance = relative + jnp.where(block < live, block * STRIPE, far_away)
            masks.append((distance >= 0) & (distance < window_len))
        return jnp.concatenate(masks, 0)

    def head_cols(head):
        return pl.ds(head * STRIPE, STRIPE)

    def masked_scores(key_rows, visible, head):
        scores = dot(key_rows, q_ref[head_cols(head)], 1, 1) * to_log2
        return jnp.where(visible, scores, neg_big)

    def add_stats(turn, carry):
        key_rows = rows_at(offsets_of(turn), 0)
        visible = visible_at(turn)
        for head in range(heads):
            cols = head_cols(head)
            scores = masked_scores(key_rows, visible, head)
            old_max = run_max[:, cols]
            new_max = jnp.maximum(old_max, jnp.max(scores, axis=0, keepdims=True))
            part = jnp.exp2(scores - new_max)
            summed = jnp.sum(part.reshape(-1, 8, STRIPE), axis=0)
            run_sum[:, cols] = run_sum[:, cols] * jnp.exp2(old_max - new_max) + summed
            run_max[:, cols] = new_max
            if keep:
                probs[turn, :, cols] = part
                tops[turn, :, cols] = new_max
        return carry

    lax.fori_loop(0, turns, add_stats, 0)
    total = jnp.sum(run_sum[...], axis=0, keepdims=True)
    run_sum[pl.ds(0, 1)] = 1.0 / total

    def add_grads(turn, carry):
        offsets = offsets_of(turn)
        key_rows, value_rows = rows_at(offsets, 0), rows_at(offsets, STRIPE)
        if not keep:
            visible = visible_at(turn)
        for head in range(heads):
            cols = head_cols(head)
            if keep:
                factor = jnp.exp2(tops[turn, :, cols] - run_max[:, cols]) * run_sum[pl.ds(0, 1), cols]
                weights = probs[turn, :, cols] * factor
            else:
                scores = masked_scores(key_rows, visible, head)
                weights = jnp.exp2(scores - run_max[:, cols]) * run_sum[pl.ds(0, 1), cols]
            weight_grad = dot(value_rows, g_ref[cols], 1, 1)
            score_grad = weights * (weight_grad - delta_ref[:, cols])
            weight_buf[:, cols] = weights.astype(jnp.bfloat16)
            grad_buf[:, cols] = score_grad.astype(jnp.bfloat16)
        score_grads = grad_buf[...]
        dq_ref[...] += dot(key_rows, score_grads, 0, 0)
        key_part = (dot(score_grads, q_ref[...], 1, 0) * inv_scale).astype(jnp.bfloat16)
        value_part = dot(weight_buf[...], g_ref[...], 1, 0).astype(jnp.bfloat16)
        for i, offset in enumerate(offsets):
            part = slice(i * STRIPE, (i + 1) * STRIPE)
            spans = [(0, half_rows, own_out)] + [
                (half_rows + j * piece_rows, piece_rows, ref) for j, ref in enumerate(other_out)
            ]
            for start, length, ref in spans:

                @pl.when((offset >= start) & (offset < start + length))
                def _(start=start, ref=ref):
                    inner = pl.multiple_of(offset - start, PAIR)
                    ref[pl.ds(inner, STRIPE)] = key_part[part]
                    ref[pl.ds(inner + STRIPE, STRIPE)] = value_part[part]

        return carry

    lax.fori_loop(0, turns, add_grads, 0)


def turn_queries(heads, inv_scale, turned, out):
    for head in range(heads):
        cols = pl.ds(head * STRIPE, STRIPE)
        out[:, cols] = (turned[:, cols].T * inv_scale).astype(jnp.bfloat16)


def vmem_limit(nbytes):
    return pltpu.CompilerParams(vmem_limit_bytes=nbytes)


vmem_spec = pl.BlockSpec(memory_space=pltpu.VMEM)
smem_spec = pl.BlockSpec(memory_space=pltpu.SMEM)


def run_prepare(layout, heads, here, order, window, queries, exps, grads, outs):
    flat = jax.ShapeDtypeStruct((heads * STRIPE, STRIPE), jnp.bfloat16)
    return pl.pallas_call(
        functools.partial(prepare, layout, heads),
        out_shape=[
            flat,
            flat,
            jax.ShapeDtypeStruct((1, heads * STRIPE), jnp.float32),
            jax.ShapeDtypeStruct((layout.count + 4,), jnp.int32),
        ],
        in_specs=[smem_spec] * 3 + [vmem_spec] * 4,
        out_specs=[vmem_spec] * 3 + [smem_spec],
        compiler_params=vmem_limit(24 * STRIPE * heads * STRIPE * 2),
        name="prep",
    )(here, order, window, queries, exps, grads, outs)


def run_attend(meta, q_flat, g_flat, delta, held, stripes, heads, inv_scale):
    pieces = len(held) // 2
    wide = q_flat.shape[0]
    turns = stripes // 2 + 1
    keep = turns * PAIR * wide * 4 <= keep_bytes
    kept = turns if keep else 1
    half_rows = stripes // 2 * PAIR
    other = jax.ShapeDtypeStruct((half_rows // pieces, STRIPE), jnp.bfloat16)
    limit = kept * PAIR * wide * 4 + 3 * 2 * half_rows * STRIPE * 2 + 10 * PAIR * wide * 2
    return pl.pallas_call(
        functools.partial(attend, stripes, pieces, heads, keep, inv_scale),
        out_shape=[
            jax.ShapeDtypeStruct((STRIPE, wide), jnp.float32),
            jax.ShapeDtypeStruct((half_rows, STRIPE), jnp.bfloat16),
        ]
        + [other] * pieces,
        in_specs=[smem_spec] + [vmem_spec] * (3 + len(held)),
        out_specs=[vmem_spec] * (2 + pieces),
        scratch_shapes=[
            pltpu.VMEM((2 * half_rows + PAIR, STRIPE), jnp.bfloat16),
            pltpu.VMEM((kept, PAIR, wide), jnp.float32),
            pltpu.VMEM((kept, 1, wide), jnp.float32),
            pltpu.VMEM((PAIR, wide), jnp.bfloat16),
            pltpu.VMEM((PAIR, wide), jnp.bfloat16),
            pltpu.VMEM((1, wide), jnp.float32),
            pltpu.VMEM((8, wide), jnp.float32),
        ],
        compiler_params=vmem_limit(limit),
        name="attend",
    )(meta, q_flat, g_flat, delta, *held)


def run_turn(turned, heads, inv_scale):
    return pl.pallas_call(
        functools.partial(turn_queries, heads, inv_scale),
        out_shape=jax.ShapeDtypeStruct(turned.shape, jnp.bfloat16),
        in_specs=[vmem_spec],
        out_specs=vmem_spec,
        compiler_params=vmem_limit(24 * STRIPE * heads * STRIPE * 2),
        name="turn",
    )(turned)


def per_device(
    layout,
    queries, query_exps, key_head, value_head, forward_out, output_grad, stripe_order, window_size
):
    head_dim = key_head.shape[1]
    tokens, feat_width = queries.shape
    heads = feat_width // head_dim
    inv_scale = 1.0 / math.sqrt(head_dim)
    stripes = layout.count
    row, col = lax.axis_index("row"), lax.axis_index("col")

    def send(value, **where):
        return lax.ppermute(value, AXES, layout.hop(**where))

    def widen(value):
        return value.astype(jnp.float32)

    pair = jnp.concatenate([key_head, value_head], 0)
    stage = [pair] + [send(pair, first=i) for i in range(1, layout.near)]
    plane = jnp.concatenate(stage, 0)
    own_pieces = [plane] + [send(plane, second=j) for j in range(1, layout.far)]
    other_pieces = [send(piece, core_flip=1) for piece in own_pieces]

    here = jnp.stack([row, col]).astype(jnp.int32)
    q_flat, g_flat, delta, meta = run_prepare(
        layout, heads, here, stripe_order, window_size,
        queries, query_exps.reshape(1, -1), output_grad, forward_out,
    )
    results = run_attend(
        meta, q_flat, g_flat, delta, own_pieces + other_pieces, stripes, heads, inv_scale
    )
    turned, own_part, other_parts = results[0], results[1], results[2:]
    query_grad = run_turn(turned, heads, inv_scale)

    piece_rows = plane.shape[0]
    summed = [
        widen(own_part[j * piece_rows : (j + 1) * piece_rows])
        + widen(send(other_parts[j], core_flip=1))
        for j in range(layout.far)
    ]
    plane_sum = summed[0]
    for j in range(1, layout.far):
        plane_sum = plane_sum + widen(send(summed[j].astype(jnp.bfloat16), second=j))
    pair_sum = plane_sum[:PAIR]
    for i in range(1, layout.near):
        part = plane_sum[i * PAIR : (i + 1) * PAIR].astype(jnp.bfloat16)
        pair_sum = pair_sum + widen(send(part, first=i))
    pair_sum = pair_sum.astype(jnp.bfloat16)
    return (query_grad, pair_sum[:tokens], pair_sum[tokens:])


def solution(mesh):
    layout = Layout(mesh.shape["row"], mesh.shape["col"])

    def whole(*arrays):
        return per_device(layout, *arrays)

    return jax.shard_map(
        whole,
        mesh=mesh,
        in_specs=(
            P(("row", "col"), None),
            P(("row", "col")),
            P(("col", "row"), None),
            P(("col", "row"), None),
            P(("row", "col"), None),
            P(("row", "col"), None),
            P(),
            P(),
        ),
        out_specs=(P(("row", "col"), None), P(("col", "row"), None), P(("col", "row"), None)),
        check_vma=False,
    )
```

```python
import functools
import math

import jax
import jax.numpy as jnp
from jax import lax
from jax.experimental import pallas as pl
from jax.experimental.pallas import tpu as pltpu
from jax.sharding import PartitionSpec as P

STRIPE = 128
PAIR = 2 * STRIPE
AXES = ("row", "col")
neg_big = -1e30
far_away = 1 << 29
keep_bytes = 24 << 20


class Layout:
    def __init__(self, rows, cols):
        self.rows, self.cols = rows, cols
        self.near, self.far = rows * 2, cols // 4
        self.square = self.near == self.far
        self.count = rows * cols

    def split(self, row, col):
        ring = col // 4
        half = ring // 2
        return row * 2 + (ring + half) % 2, half * 2 + (col // 2) % 2, col % 2

    def join(self, near, far, core):
        half = far // 2
        ring = half * 2 + (near + half) % 2
        return (near // 2) * self.cols + ring * 4 + (far % 2) * 2 + core

    def hop(self, first=0, second=0, core_flip=0):
        pairs = []
        for device in range(self.count):
            near, far, core = self.split(device // self.cols, device % self.cols)
            if self.square and core == 1:
                near, far = near ^ second, far ^ first
            else:
                near, far = near ^ first, far ^ second
            pairs.append((device, self.join(near, far, core ^ core_flip)))
        return pairs

    def slot(self, own, stored):
        near, far, core = self.split(stored % self.rows, stored // self.rows)
        near, far = near ^ own[0], far ^ own[1]
        place = far * self.near + near
        if self.square:
            place = jnp.where(core == 1, near * self.far + far, place)
        return place + jnp.where(core == own[2], 0, self.count // 2)


def dot(left, right, left_dim, right_dim):
    return lax.dot_general(
        left, right, (((left_dim,), (right_dim,)), ((), ())), preferred_element_type=jnp.float32
    )


def prepare(layout, heads, here, order, window, q_ref, e_ref, g_ref, o_ref, q_out, g_out, d_out, meta):
    row, col = here[0], here[1]
    own = layout.split(row, col)
    own_block = order[row * layout.cols + col]
    live = jnp.minimum(own_block, (window[0] + STRIPE - 2) // STRIPE) + 1
    meta[0] = live
    meta[1] = window[0]

    def clear(back, carry):
        meta[2 + back] = layout.count * PAIR
        return carry

    def place(stored, carry):
        back = own_block - order[stored]

        @pl.when((back >= 0) & (back < live))
        def _():
            meta[2 + back] = layout.slot(own, stored) * PAIR

        return carry

    lax.fori_loop(0, layout.count + 2, clear, 0)
    lax.fori_loop(0, layout.count, place, 0)
    power = jnp.left_shift(1, e_ref[...] + 1).astype(jnp.float32) * 0.5
    power = jnp.broadcast_to(power, (STRIPE, STRIPE)).T
    for head in range(heads):
        cols = pl.ds(head * STRIPE, STRIPE)
        q_out[cols] = (q_ref[:, cols].astype(jnp.float32) * power).astype(jnp.bfloat16)
        grads = g_ref[:, cols]
        g_out[cols] = grads
        product = grads.astype(jnp.float32) * o_ref[:, cols].astype(jnp.float32)
        sums = jnp.sum(product.T, axis=0, keepdims=True)
        d_out[:, cols] = sums.astype(jnp.bfloat16).astype(jnp.float32)


def attend(
    stripes, pieces, heads, keep, inv_scale,
    meta, q_ref, g_ref, delta_ref, *refs,
):
    held, rest = refs[: 2 * pieces], refs[2 * pieces :]
    dq_ref, own_out, other_out, rest = rest[0], rest[1], rest[2 : 2 + pieces], rest[2 + pieces :]
    kv, probs, weight_a, weight_b, grad_a, grad_b, run_max, run_sum, top, inverse = rest
    half_rows = stripes // 2 * PAIR
    piece_rows = half_rows // pieces
    to_log2 = inv_scale * math.log2(math.e)
    live, window_len = meta[0], meta[1]
    turns = (live + 1) // 2
    last_whole = jnp.minimum(live - 1, (window_len - STRIPE) // STRIPE)
    middle = jnp.maximum((last_whole + 1) // 2, 1)

    for i, ref in enumerate(held):
        kv[pl.ds(i * piece_rows, piece_rows)] = ref[...]
    kv[pl.ds(2 * half_rows, PAIR)] = jnp.zeros((PAIR, STRIPE), kv.dtype)
    for ref in (own_out, *other_out):
        ref[...] = jnp.zeros_like(ref)
    run_max[...] = jnp.full_like(run_max, neg_big)
    run_sum[...] = jnp.zeros_like(run_sum)
    dq_ref[...] = jnp.zeros_like(dq_ref)

    group = 2 if heads % 2 == 0 else 1
    wide = group * STRIPE
    groups = [pl.ds(i * wide, wide) for i in range(heads // group)]

    def offsets_of(turn):
        return [pl.multiple_of(meta[2 + 2 * turn + i], PAIR) for i in range(2)]

    def rows_at(turn, shift):
        return jnp.concatenate([kv[pl.ds(offset + shift, STRIPE)] for offset in offsets_of(turn)], 0)

    def visible_at(turn):
        relative = lax.broadcasted_iota(jnp.int32, (STRIPE, STRIPE), 1) - lax.broadcasted_iota(
            jnp.int32, (STRIPE, STRIPE), 0
        )
        masks = []
        for i in range(2):
            block = 2 * turn + i
            distance = relative + jnp.where(block < live, block * STRIPE, far_away)
            masks.append((distance >= 0) & (distance < window_len))
        mask = jnp.concatenate(masks, 0)
        return jnp.concatenate([mask] * group, 1)

    def scores_of(key_rows, visible, cols):
        scores = dot(key_rows, q_ref[cols], 1, 1)
        return scores if visible is None else jnp.where(visible, scores, neg_big)

    def by_eight(value):
        return value.reshape(-1, 8, value.shape[1])

    def find_max(turn, visible):
        key_rows = rows_at(turn, 0)
        for cols in groups:
            scores = scores_of(key_rows, visible, cols)
            run_max[:, cols] = jnp.maximum(run_max[:, cols], jnp.max(by_eight(scores), axis=0))
            if keep:
                probs[turn, :, cols] = scores

    def masked_max(turn, carry):
        find_max(turn, visible_at(turn))
        return carry

    def plain_max(turn, carry):
        find_max(turn, None)
        return carry

    lax.fori_loop(0, 1, masked_max, 0)
    lax.fori_loop(1, middle, plain_max, 0)
    lax.fori_loop(middle, turns, masked_max, 0)
    top[...] = jnp.max(run_max[...], axis=0, keepdims=True) * to_log2

    def exponentials(turn, cols):
        if keep:
            scores = probs[turn, :, cols]
        else:
            scores = scores_of(rows_at(turn, 0), visible_at(turn), cols)
        return jnp.exp2(scores * to_log2 - top[:, cols])

    def add_sums(turn, carry):
        for cols in groups:
            part = exponentials(turn, cols)
            run_sum[:, cols] += jnp.sum(by_eight(part), axis=0)
            if keep:
                probs[turn, :, cols] = part
        return carry

    lax.fori_loop(0, turns, add_sums, 0)
    inverse[...] = 1.0 / jnp.sum(run_sum[...], axis=0, keepdims=True)

    def find_grads(turn, weight_buf, grad_buf):
        value_rows = rows_at(turn, STRIPE)
        for cols in groups:
            part = probs[turn, :, cols] if keep else exponentials(turn, cols)
            weights = part * inverse[:, cols]
            weight_grad = dot(value_rows, g_ref[cols], 1, 1)
            score_grad = weights * (weight_grad - delta_ref[:, cols])
            weight_buf[:, cols] = weights.astype(jnp.bfloat16)
            grad_buf[:, cols] = score_grad.astype(jnp.bfloat16)

    def products(turn, weight_buf, grad_buf):
        score_grads = grad_buf[...]
        dq_ref[...] += dot(rows_at(turn, 0), score_grads, 0, 0)
        key_part = (dot(score_grads, q_ref[...], 1, 0) * inv_scale).astype(jnp.bfloat16)
        value_part = dot(weight_buf[...], g_ref[...], 1, 0).astype(jnp.bfloat16)
        return key_part, value_part

    def store(turn, parts):
        spans = [(0, half_rows, own_out)] + [
            (half_rows + j * piece_rows, piece_rows, ref) for j, ref in enumerate(other_out)
        ]
        for i, offset in enumerate(offsets_of(turn)):
            rows = slice(i * STRIPE, (i + 1) * STRIPE)
            for start, length, ref in spans:

                @pl.when((offset >= start) & (offset < start + length))
                def _(start=start, ref=ref):
                    inner = pl.multiple_of(offset - start, PAIR)
                    for j, part in enumerate(parts):
                        ref[pl.ds(inner + j * STRIPE, STRIPE)] = part[rows]

    a, b = (weight_a, grad_a), (weight_b, grad_b)

    def step(turn, now, before):
        parts = products(turn - 1, *before)
        find_grads(turn, *now)
        store(turn - 1, parts)

    def two_steps(pair, carry):
        step(2 * pair + 1, b, a)
        step(2 * pair + 2, a, b)
        return carry

    find_grads(0, *a)
    lax.fori_loop(0, (turns - 1) // 2, two_steps, 0)

    @pl.when(turns % 2 == 0)
    def _():
        step(turns - 1, b, a)
        store(turns - 1, products(turns - 1, *b))

    @pl.when(turns % 2 == 1)
    def _():
        store(turns - 1, products(turns - 1, *a))


def turn_queries(heads, inv_scale, turned, out):
    for head in range(heads):
        cols = pl.ds(head * STRIPE, STRIPE)
        out[:, cols] = (turned[:, cols].T * inv_scale).astype(jnp.bfloat16)


def vmem_limit(nbytes):
    return pltpu.CompilerParams(vmem_limit_bytes=nbytes)


vmem_spec = pl.BlockSpec(memory_space=pltpu.VMEM)
smem_spec = pl.BlockSpec(memory_space=pltpu.SMEM)


def run_prepare(layout, heads, here, order, window, queries, exps, grads, outs):
    flat = jax.ShapeDtypeStruct((heads * STRIPE, STRIPE), jnp.bfloat16)
    return pl.pallas_call(
        functools.partial(prepare, layout, heads),
        out_shape=[
            flat,
            flat,
            jax.ShapeDtypeStruct((1, heads * STRIPE), jnp.float32),
            jax.ShapeDtypeStruct((layout.count + 4,), jnp.int32),
        ],
        in_specs=[smem_spec] * 3 + [vmem_spec] * 4,
        out_specs=[vmem_spec] * 3 + [smem_spec],
        compiler_params=vmem_limit(24 * STRIPE * heads * STRIPE * 2),
        name="prep",
    )(here, order, window, queries, exps, grads, outs)


def run_attend(meta, q_flat, g_flat, delta, held, stripes, heads, inv_scale):
    pieces = len(held) // 2
    wide = q_flat.shape[0]
    turns = stripes // 2 + 1
    keep = turns * PAIR * wide * 4 <= keep_bytes
    kept = turns if keep else 1
    half_rows = stripes // 2 * PAIR
    other = jax.ShapeDtypeStruct((half_rows // pieces, STRIPE), jnp.bfloat16)
    limit = kept * PAIR * wide * 4 + 3 * 2 * half_rows * STRIPE * 2 + 10 * PAIR * wide * 2
    return pl.pallas_call(
        functools.partial(attend, stripes, pieces, heads, keep, inv_scale),
        out_shape=[
            jax.ShapeDtypeStruct((STRIPE, wide), jnp.float32),
            jax.ShapeDtypeStruct((half_rows, STRIPE), jnp.bfloat16),
        ]
        + [other] * pieces,
        in_specs=[smem_spec] + [vmem_spec] * (3 + len(held)),
        out_specs=[vmem_spec] * (2 + pieces),
        scratch_shapes=[
            pltpu.VMEM((2 * half_rows + PAIR, STRIPE), jnp.bfloat16),
            pltpu.VMEM((kept, PAIR, wide), jnp.float32),
            *[pltpu.VMEM((PAIR, wide), jnp.bfloat16)] * 4,
            *[pltpu.VMEM((8, wide), jnp.float32)] * 2,
            *[pltpu.VMEM((1, wide), jnp.float32)] * 2,
        ],
        compiler_params=vmem_limit(limit),
        name="attend",
    )(meta, q_flat, g_flat, delta, *held)


def run_turn(turned, heads, inv_scale):
    return pl.pallas_call(
        functools.partial(turn_queries, heads, inv_scale),
        out_shape=jax.ShapeDtypeStruct(turned.shape, jnp.bfloat16),
        in_specs=[vmem_spec],
        out_specs=vmem_spec,
        compiler_params=vmem_limit(24 * STRIPE * heads * STRIPE * 2),
        name="turn",
    )(turned)


def per_device(
    layout,
    queries, query_exps, key_head, value_head, forward_out, output_grad, stripe_order, window_size
):
    head_dim = key_head.shape[1]
    tokens, feat_width = queries.shape
    heads = feat_width // head_dim
    inv_scale = 1.0 / math.sqrt(head_dim)
    stripes = layout.count
    row, col = lax.axis_index("row"), lax.axis_index("col")

    def send(value, **where):
        return lax.ppermute(value, AXES, layout.hop(**where))

    def widen(value):
        return value.astype(jnp.float32)

    pair = jnp.concatenate([key_head, value_head], 0)
    stage = [pair] + [send(pair, first=i) for i in range(1, layout.near)]
    plane = jnp.concatenate(stage, 0)
    own_pieces = [plane] + [send(plane, second=j) for j in range(1, layout.far)]
    other_pieces = [send(piece, core_flip=1) for piece in own_pieces]

    here = jnp.stack([row, col]).astype(jnp.int32)
    q_flat, g_flat, delta, meta = run_prepare(
        layout, heads, here, stripe_order, window_size,
        queries, query_exps.reshape(1, -1), output_grad, forward_out,
    )
    results = run_attend(
        meta, q_flat, g_flat, delta, own_pieces + other_pieces, stripes, heads, inv_scale
    )
    turned, own_part, other_parts = results[0], results[1], results[2:]
    query_grad = run_turn(turned, heads, inv_scale)

    piece_rows = plane.shape[0]
    summed = [
        widen(own_part[j * piece_rows : (j + 1) * piece_rows])
        + widen(send(other_parts[j], core_flip=1))
        for j in range(layout.far)
    ]
    plane_sum = summed[0]
    for j in range(1, layout.far):
        plane_sum = plane_sum + widen(send(summed[j].astype(jnp.bfloat16), second=j))
    pair_sum = plane_sum[:PAIR]
    for i in range(1, layout.near):
        part = plane_sum[i * PAIR : (i + 1) * PAIR].astype(jnp.bfloat16)
        pair_sum = pair_sum + widen(send(part, first=i))
    pair_sum = pair_sum.astype(jnp.bfloat16)
    return (query_grad, pair_sum[:tokens], pair_sum[tokens:])


def solution(mesh):
    layout = Layout(mesh.shape["row"], mesh.shape["col"])

    def whole(*arrays):
        return per_device(layout, *arrays)

    return jax.shard_map(
        whole,
        mesh=mesh,
        in_specs=(
            P(("row", "col"), None),
            P(("row", "col")),
            P(("col", "row"), None),
            P(("col", "row"), None),
            P(("row", "col"), None),
            P(("row", "col"), None),
            P(),
            P(),
        ),
        out_specs=(P(("row", "col"), None), P(("col", "row"), None), P(("col", "row"), None)),
        check_vma=False,
    )
```

```python
import functools
import math

import jax
import jax.numpy as jnp
from jax import lax
from jax.experimental import pallas as pl
from jax.experimental.pallas import tpu as pltpu
from jax.sharding import PartitionSpec as P

STRIPE = 128
PAIR = 2 * STRIPE
AXES = ("row", "col")
neg_big = -1e30
far_blocks = 1 << 22
head_len = 3
keep_bytes = 24 << 20


class Layout:
    def __init__(self, rows, cols):
        self.rows, self.cols = rows, cols
        self.near, self.far = rows * 2, cols // 4
        self.square = self.near == self.far
        self.count = rows * cols

    def split(self, row, col):
        ring = col // 4
        half = ring // 2
        return row * 2 + (ring + half) % 2, half * 2 + (col // 2) % 2, col % 2

    def join(self, near, far, core):
        half = far // 2
        ring = half * 2 + (near + half) % 2
        return (near // 2) * self.cols + ring * 4 + (far % 2) * 2 + core

    def hop(self, first=0, second=0, core_flip=0):
        pairs = []
        for device in range(self.count):
            near, far, core = self.split(device // self.cols, device % self.cols)
            if self.square and core == 1:
                near, far = near ^ second, far ^ first
            else:
                near, far = near ^ first, far ^ second
            pairs.append((device, self.join(near, far, core ^ core_flip)))
        return pairs

    def slot(self, own, stored):
        near, far, core = self.split(stored % self.rows, stored // self.rows)
        near, far = near ^ own[0], far ^ own[1]
        place = far * self.near + near
        if self.square:
            place = jnp.where(core == 1, near * self.far + far, place)
        return place + jnp.where(core == own[2], 0, self.count // 2)

    def early(self, slot):
        return slot % (self.count // 2) >= self.count // 4


def dot(left, right, left_dim, right_dim):
    return lax.dot_general(
        left, right, (((left_dim,), (right_dim,)), ((), ())), preferred_element_type=jnp.float32
    )


def prepare(
    layout, heads, here, order, window, q_ref, e_ref, g_ref, o_ref, q_out, g_out, d_out, meta
):
    row, col = here[0], here[1]
    own = layout.split(row, col)
    own_block = order[row * layout.cols + col]
    live = jnp.minimum(own_block, (window[0] + STRIPE - 2) // STRIPE) + 1
    part_len = layout.count + 2

    def write(part, place, slot, back):
        start = head_len + part * part_len + 2 * place
        meta[start] = slot
        meta[start + 1] = back

    def visit(stored, filled):
        back = own_block - order[stored]
        slot = layout.slot(own, stored)
        early = layout.early(slot)
        wanted = (back >= 0) & (back < live)

        @pl.when(wanted)
        def _():
            write(jnp.where(early, 0, 1), jnp.where(early, filled[0], filled[1]), slot, back)

        return (
            filled[0] + (wanted & early).astype(jnp.int32),
            filled[1] + (wanted & jnp.logical_not(early)).astype(jnp.int32),
        )

    filled = lax.fori_loop(0, layout.count, visit, (jnp.int32(0), jnp.int32(0)))
    turns = [(count + 1) // 2 for count in filled]
    for part, count in enumerate(filled):
        write(part, count, layout.count, far_blocks)
    meta[0] = turns[0]
    meta[1] = turns[0] + turns[1]
    meta[2] = window[0]
    power = jnp.left_shift(1, e_ref[...] + 1).astype(jnp.float32) * 0.5
    power = jnp.broadcast_to(power, (STRIPE, STRIPE)).T
    for head in range(heads):
        cols = pl.ds(head * STRIPE, STRIPE)
        q_out[cols] = (q_ref[:, cols].astype(jnp.float32) * power).astype(jnp.bfloat16)
        grads = g_ref[:, cols]
        g_out[cols] = grads
        product = grads.astype(jnp.float32) * o_ref[:, cols].astype(jnp.float32)
        sums = jnp.sum(product.T, axis=0, keepdims=True)
        d_out[:, cols] = sums.astype(jnp.bfloat16).astype(jnp.float32)


def blocks_of(meta, turn):
    part_len = (meta.shape[0] - head_len) // 2
    early = meta[0]
    start = head_len + jnp.where(turn < early, 4 * turn, part_len + 4 * (turn - early))
    return [meta[start], meta[start + 2]], [meta[start + 1], meta[start + 3]]


def rows_at(meta, kv, turn, shift):
    slots, _ = blocks_of(meta, turn)
    return jnp.concatenate(
        [kv[pl.ds(pl.multiple_of(slot * PAIR, PAIR) + shift, STRIPE)] for slot in slots], 0
    )


def visible_at(meta, turn):
    relative = lax.broadcasted_iota(jnp.int32, (STRIPE, STRIPE), 1) - lax.broadcasted_iota(
        jnp.int32, (STRIPE, STRIPE), 0
    )
    _, backs = blocks_of(meta, turn)
    distances = [relative + back * STRIPE for back in backs]
    return jnp.concatenate([(d >= 0) & (d < meta[2]) for d in distances], 0)


def groups_of(heads):
    group = 2 if heads % 2 == 0 else 1
    wide = group * STRIPE
    return group, [pl.ds(i * wide, wide) for i in range(heads // group)]


def masked_scores(meta, q_ref, kv, turn, cols, group):
    scores = dot(rows_at(meta, kv, turn, 0), q_ref[cols], 1, 1)
    visible = jnp.concatenate([visible_at(meta, turn)] * group, 1)
    return jnp.where(visible, scores, neg_big)


def by_eight(value):
    return value.reshape(-1, 8, value.shape[1])


def find_weights(heads, keep, to_log2, meta, q_ref, kv, probs, run_max, run_sum, top, inverse):
    group, groups = groups_of(heads)
    turns, window_len = meta[1], meta[2]
    run_max[...] = jnp.full_like(run_max, neg_big)
    run_sum[...] = jnp.zeros_like(run_sum)

    def find_max(turn, masked):
        key_rows = rows_at(meta, kv, turn, 0)
        if masked:
            visible = jnp.concatenate([visible_at(meta, turn)] * group, 1)
        for cols in groups:
            scores = dot(key_rows, q_ref[cols], 1, 1)
            if masked:
                scores = jnp.where(visible, scores, neg_big)
            run_max[:, cols] = jnp.maximum(run_max[:, cols], jnp.max(by_eight(scores), axis=0))
            if keep:
                probs[turn, :, cols] = scores

    def add_max(turn, carry):
        _, backs = blocks_of(meta, turn)
        nearest, farthest = jnp.minimum(*backs), jnp.maximum(*backs)
        whole = (nearest >= 1) & (farthest * STRIPE + (STRIPE - 1) < window_len)

        @pl.when(whole)
        def _():
            find_max(turn, False)

        @pl.when(jnp.logical_not(whole))
        def _():
            find_max(turn, True)

        return carry

    lax.fori_loop(0, turns, add_max, 0)
    top[...] = jnp.max(run_max[...], axis=0, keepdims=True) * to_log2

    def add_sums(turn, carry):
        for cols in groups:
            if keep:
                scores = probs[turn, :, cols]
            else:
                scores = masked_scores(meta, q_ref, kv, turn, cols, group)
            part = jnp.exp2(scores * to_log2 - top[:, cols])
            run_sum[:, cols] += jnp.sum(by_eight(part), axis=0)
            if keep:
                probs[turn, :, cols] = part
        return carry

    lax.fori_loop(0, turns, add_sums, 0)
    inverse[...] = 1.0 / jnp.sum(run_sum[...], axis=0, keepdims=True)


def add_gradients(
    heads, keep, inv_scale, meta, begin, end,
    q_ref, g_ref, delta_ref, kv, probs, top, inverse, dq_ref, outs, buffers,
):
    group, groups = groups_of(heads)
    to_log2 = inv_scale * math.log2(math.e)

    def find_grads(turn, weight_buf, grad_buf):
        value_rows = rows_at(meta, kv, turn, STRIPE)
        for cols in groups:
            if keep:
                part = probs[turn, :, cols]
            else:
                scores = masked_scores(meta, q_ref, kv, turn, cols, group)
                part = jnp.exp2(scores * to_log2 - top[:, cols])
            weights = part * inverse[:, cols]
            weight_grad = dot(value_rows, g_ref[cols], 1, 1)
            score_grad = weights * (weight_grad - delta_ref[:, cols])
            weight_buf[:, cols] = weights.astype(jnp.bfloat16)
            grad_buf[:, cols] = score_grad.astype(jnp.bfloat16)

    def products(turn, weight_buf, grad_buf):
        score_grads = grad_buf[...]
        dq_ref[...] += dot(rows_at(meta, kv, turn, 0), score_grads, 0, 0)
        key_part = (dot(score_grads, q_ref[...], 1, 0) * inv_scale).astype(jnp.bfloat16)
        value_part = dot(weight_buf[...], g_ref[...], 1, 0).astype(jnp.bfloat16)
        return key_part, value_part

    def store(turn, parts):
        slots, _ = blocks_of(meta, turn)
        for i, slot in enumerate(slots):
            rows = slice(i * STRIPE, (i + 1) * STRIPE)
            for start, ref in outs:

                @pl.when((slot >= start) & (slot < start + ref.shape[0] // PAIR))
                def _(start=start, ref=ref):
                    inner = pl.multiple_of((slot - start) * PAIR, PAIR)
                    for j, part in enumerate(parts):
                        ref[pl.ds(inner + j * STRIPE, STRIPE)] = part[rows]

    for _, ref in outs:
        ref[...] = jnp.zeros_like(ref)
    weight_a, weight_b, grad_a, grad_b = buffers
    a, b = (weight_a, grad_a), (weight_b, grad_b)
    last = end - 1
    pairs = jnp.maximum(last - begin, 0) // 2

    def step(turn, now, before):
        parts = products(turn - 1, *before)
        find_grads(turn, *now)
        store(turn - 1, parts)

    def two_steps(pair, carry):
        turn = begin + 2 * pair
        step(turn + 1, b, a)
        step(turn + 2, a, b)
        return carry

    @pl.when(end > begin)
    def _():
        find_grads(begin, *a)
        lax.fori_loop(0, pairs, two_steps, 0)

    @pl.when((end > begin) & ((end - begin) % 2 == 0))
    def _():
        step(last, b, a)
        store(last, products(last, *b))

    @pl.when((end > begin) & ((end - begin) % 2 == 1))
    def _():
        store(last, products(last, *a))


def spans_of(stripes, pieces, refs, first_piece):
    length = stripes // 2 // pieces
    half = len(refs) // 2
    own = [((first_piece + i) * length, ref) for i, ref in enumerate(refs[:half])]
    other = [
        (stripes // 2 + (first_piece + i) * length, ref) for i, ref in enumerate(refs[half:])
    ]
    return own + other


def attend_early(stripes, pieces, heads, keep, inv_scale, meta, q_ref, g_ref, delta_ref, *refs):
    held, rest = refs[: 2 * pieces], refs[2 * pieces :]
    kv, probs, top, inverse, dq_ref, rest = *rest[:5], rest[5:]
    outs, rest = rest[:pieces], rest[pieces:]
    run_max, run_sum, *buffers = rest
    rows = held[0].shape[0]
    for i, piece in enumerate(held):
        kv[pl.ds(i * rows, rows)] = piece[...]
    kv[pl.ds(len(held) * rows, PAIR)] = jnp.zeros((PAIR, STRIPE), kv.dtype)
    dq_ref[...] = jnp.zeros_like(dq_ref)
    to_log2 = inv_scale * math.log2(math.e)
    find_weights(heads, keep, to_log2, meta, q_ref, kv, probs, run_max, run_sum, top, inverse)
    add_gradients(
        heads, keep, inv_scale, meta, 0, meta[0],
        q_ref, g_ref, delta_ref, kv, probs, top, inverse, dq_ref,
        spans_of(stripes, pieces, outs, pieces // 2), buffers,
    )


def attend_late(
    stripes, pieces, heads, keep, inv_scale,
    meta, q_ref, g_ref, delta_ref, kv, probs, top, inverse, dq_early, dq_ref, *refs,
):
    outs, buffers = refs[:pieces], refs[pieces:]
    dq_ref[...] = dq_early[...]
    add_gradients(
        heads, keep, inv_scale, meta, meta[0], meta[1],
        q_ref, g_ref, delta_ref, kv, probs, top, inverse, dq_ref,
        spans_of(stripes, pieces, outs, 0), buffers,
    )


def turn_queries(heads, inv_scale, turned, out):
    for head in range(heads):
        cols = pl.ds(head * STRIPE, STRIPE)
        out[:, cols] = (turned[:, cols].T * inv_scale).astype(jnp.bfloat16)


def vmem_limit(nbytes):
    return pltpu.CompilerParams(vmem_limit_bytes=nbytes)


vmem_spec = pl.BlockSpec(memory_space=pltpu.VMEM)
smem_spec = pl.BlockSpec(memory_space=pltpu.SMEM)


def run_prepare(layout, heads, here, order, window, queries, exps, grads, outs):
    flat = jax.ShapeDtypeStruct((heads * STRIPE, STRIPE), jnp.bfloat16)
    return pl.pallas_call(
        functools.partial(prepare, layout, heads),
        out_shape=[
            flat,
            flat,
            jax.ShapeDtypeStruct((1, heads * STRIPE), jnp.float32),
            jax.ShapeDtypeStruct((head_len + 2 * (layout.count + 2),), jnp.int32),
        ],
        in_specs=[smem_spec] * 3 + [vmem_spec] * 4,
        out_specs=[vmem_spec] * 3 + [smem_spec],
        compiler_params=vmem_limit(24 * STRIPE * heads * STRIPE * 2),
        name="prep",
    )(here, order, window, queries, exps, grads, outs)


def run_attend(early, meta, q_flat, g_flat, delta, others, pieces, stripes, heads, inv_scale):
    wide = q_flat.shape[0]
    turns = stripes // 2 + 2
    keep = turns * PAIR * wide * 4 <= keep_bytes
    half_rows = stripes // 2 * PAIR
    query_sum = jax.ShapeDtypeStruct((STRIPE, wide), jnp.float32)
    row = jax.ShapeDtypeStruct((1, wide), jnp.float32)
    outs = [query_sum] + [
        jax.ShapeDtypeStruct((half_rows // pieces, STRIPE), jnp.bfloat16)
    ] * pieces
    scratch = [pltpu.VMEM((PAIR, wide), jnp.bfloat16)] * 4
    if early:
        outs = [
            jax.ShapeDtypeStruct((2 * half_rows + PAIR, STRIPE), jnp.bfloat16),
            jax.ShapeDtypeStruct((turns if keep else 1, PAIR, wide), jnp.float32),
            row,
            row,
        ] + outs
        scratch = [pltpu.VMEM((8, wide), jnp.float32)] * 2 + scratch
    body = attend_early if early else attend_late
    return pl.pallas_call(
        functools.partial(body, stripes, pieces, heads, keep, inv_scale),
        out_shape=outs,
        in_specs=[smem_spec] + [vmem_spec] * (3 + len(others)),
        out_specs=[vmem_spec] * len(outs),
        scratch_shapes=scratch,
        compiler_params=vmem_limit(13 * half_rows * STRIPE + 12 * PAIR * wide * 2),
        name="early" if early else "late",
    )(meta, q_flat, g_flat, delta, *others)


def run_turn(turned, heads, inv_scale):
    return pl.pallas_call(
        functools.partial(turn_queries, heads, inv_scale),
        out_shape=jax.ShapeDtypeStruct(turned.shape, jnp.bfloat16),
        in_specs=[vmem_spec],
        out_specs=vmem_spec,
        compiler_params=vmem_limit(24 * STRIPE * heads * STRIPE * 2),
        name="turn",
    )(turned)


def per_device(
    layout,
    queries, query_exps, key_head, value_head, forward_out, output_grad, stripe_order, window_size
):
    head_dim = key_head.shape[1]
    tokens, feat_width = queries.shape
    heads = feat_width // head_dim
    inv_scale = 1.0 / math.sqrt(head_dim)
    stripes = layout.count
    row, col = lax.axis_index("row"), lax.axis_index("col")

    def send(value, **where):
        return lax.ppermute(value, AXES, layout.hop(**where))

    def widen(value):
        return value.astype(jnp.float32)

    pair = jnp.concatenate([key_head, value_head], 0)
    stage = [pair] + [send(pair, first=i) for i in range(1, layout.near)]
    plane = jnp.concatenate(stage, 0)
    own_pieces = [plane] + [send(plane, second=j) for j in range(1, layout.far)]
    other_pieces = [send(piece, core_flip=1) for piece in own_pieces]

    here = jnp.stack([row, col]).astype(jnp.int32)
    q_flat, g_flat, delta, meta = run_prepare(
        layout, heads, here, stripe_order, window_size,
        queries, query_exps.reshape(1, -1), output_grad, forward_out,
    )
    pieces = layout.far
    split = pieces // 2
    results = run_attend(
        True, meta, q_flat, g_flat, delta, own_pieces + other_pieces,
        pieces, stripes, heads, inv_scale,
    )
    between, early_parts = results[:5], results[5:]
    results = run_attend(
        False, meta, q_flat, g_flat, delta, between, pieces, stripes, heads, inv_scale
    )
    turned, late_parts = results[0], results[1:]
    query_grad = run_turn(turned, heads, inv_scale)

    own_parts = late_parts[:split] + early_parts[:split]
    other_parts = late_parts[split:] + early_parts[split:]
    summed = [None] * pieces
    for j in reversed(range(pieces)):
        arrived = send(other_parts[j], core_flip=1)
        summed[j] = widen(own_parts[j]) + widen(arrived)
    plane_sum = summed[0]
    for j in range(1, pieces):
        plane_sum = plane_sum + widen(send(summed[j].astype(jnp.bfloat16), second=j))
    pair_sum = plane_sum[:PAIR]
    for i in range(1, layout.near):
        part = plane_sum[i * PAIR : (i + 1) * PAIR].astype(jnp.bfloat16)
        pair_sum = pair_sum + widen(send(part, first=i))
    pair_sum = pair_sum.astype(jnp.bfloat16)
    return (query_grad, pair_sum[:tokens], pair_sum[tokens:])


def solution(mesh):
    layout = Layout(mesh.shape["row"], mesh.shape["col"])

    def whole(*arrays):
        return per_device(layout, *arrays)

    return jax.shard_map(
        whole,
        mesh=mesh,
        in_specs=(
            P(("row", "col"), None),
            P(("row", "col")),
            P(("col", "row"), None),
            P(("col", "row"), None),
            P(("row", "col"), None),
            P(("row", "col"), None),
            P(),
            P(),
        ),
        out_specs=(P(("row", "col"), None), P(("col", "row"), None), P(("col", "row"), None)),
        check_vma=False,
    )
```

```python
import functools
import math

import jax
import jax.numpy as jnp
from jax import lax
from jax.experimental import pallas as pl
from jax.experimental.pallas import tpu as pltpu
from jax.sharding import PartitionSpec as P

STRIPE = 128
PAIR = 2 * STRIPE
AXES = ("row", "col")
neg_big = -1e30
far_blocks = 1 << 22
head_len = 3
keep_bytes = 24 << 20


class Layout:
    def __init__(self, rows, cols):
        self.rows, self.cols = rows, cols
        self.near, self.far = rows * 2, cols // 4
        self.square = self.near == self.far
        self.count = rows * cols

    def chip(self, row, col, kind):
        ring = col // 4
        half = ring // 2
        fold = half if kind == 0 else 0
        return row * 2 + (ring + fold) % 2, half * 2 + (col // 2) % 2

    def hop(self, first=0, second=0, core_flip=0):
        pairs = []
        for device in range(self.count):
            col = device % self.cols
            core = col % 2
            near, far = self.chip(device // self.cols, col, core)
            if self.square and core == 1:
                near, far = near ^ second, far ^ first
            else:
                near, far = near ^ first, far ^ second
            half = far // 2
            fold = half if core == 0 else 0
            col = (half * 2 + (near + fold) % 2) * 4 + (far % 2) * 2 + (core ^ core_flip)
            pairs.append((device, (near // 2) * self.cols + col))
        return pairs

    def slot(self, row, col, stored):
        core = (stored // self.rows) % 2
        places = []
        for kind in range(2):
            own = self.chip(row, col, kind)
            other = self.chip(stored % self.rows, stored // self.rows, kind)
            near, far = own[0] ^ other[0], own[1] ^ other[1]
            turned = self.square and kind == 1
            places.append(near * self.far + far if turned else far * self.near + near)
        place = jnp.where(core == 1, places[1], places[0])
        return place + jnp.where(core == col % 2, 0, self.count // 2)

    def early(self, slot):
        return slot % (self.count // 2) >= self.count // 4


def dot(left, right, left_dim, right_dim):
    return lax.dot_general(
        left, right, (((left_dim,), (right_dim,)), ((), ())), preferred_element_type=jnp.float32
    )


def prepare(
    layout, heads, here, order, window, q_ref, e_ref, g_ref, o_ref, q_out, g_out, d_out, meta
):
    row, col = here[0], here[1]
    own_block = order[row * layout.cols + col]
    live = jnp.minimum(own_block, (window[0] + STRIPE - 2) // STRIPE) + 1
    part_len = layout.count + 2

    def write(part, place, slot, back):
        start = head_len + part * part_len + 2 * place
        meta[start] = slot
        meta[start + 1] = back

    def visit(stored, filled):
        back = own_block - order[stored]
        slot = layout.slot(row, col, stored)
        early = layout.early(slot)
        wanted = (back >= 0) & (back < live)

        @pl.when(wanted)
        def _():
            write(jnp.where(early, 0, 1), jnp.where(early, filled[0], filled[1]), slot, back)

        return (
            filled[0] + (wanted & early).astype(jnp.int32),
            filled[1] + (wanted & jnp.logical_not(early)).astype(jnp.int32),
        )

    filled = lax.fori_loop(0, layout.count, visit, (jnp.int32(0), jnp.int32(0)))
    turns = [(count + 1) // 2 for count in filled]
    for part, count in enumerate(filled):
        write(part, count, layout.count, far_blocks)
    meta[0] = turns[0]
    meta[1] = turns[0] + turns[1]
    meta[2] = window[0]
    power = jnp.left_shift(1, e_ref[...] + 1).astype(jnp.float32) * 0.5
    power = jnp.broadcast_to(power, (STRIPE, STRIPE)).T
    for head in range(heads):
        cols = pl.ds(head * STRIPE, STRIPE)
        q_out[cols] = (q_ref[:, cols].astype(jnp.float32) * power).astype(jnp.bfloat16)
        grads = g_ref[:, cols]
        g_out[cols] = grads
        product = grads.astype(jnp.float32) * o_ref[:, cols].astype(jnp.float32)
        sums = jnp.sum(product.T, axis=0, keepdims=True)
        d_out[:, cols] = sums.astype(jnp.bfloat16).astype(jnp.float32)


def blocks_of(meta, turn):
    part_len = (meta.shape[0] - head_len) // 2
    early = meta[0]
    start = head_len + jnp.where(turn < early, 4 * turn, part_len + 4 * (turn - early))
    return [meta[start], meta[start + 2]], [meta[start + 1], meta[start + 3]]


def rows_at(meta, kv, turn, shift):
    slots, _ = blocks_of(meta, turn)
    return jnp.concatenate(
        [kv[pl.ds(pl.multiple_of(slot * PAIR, PAIR) + shift, STRIPE)] for slot in slots], 0
    )


def visible_at(meta, turn):
    relative = lax.broadcasted_iota(jnp.int32, (STRIPE, STRIPE), 1) - lax.broadcasted_iota(
        jnp.int32, (STRIPE, STRIPE), 0
    )
    _, backs = blocks_of(meta, turn)
    distances = [relative + back * STRIPE for back in backs]
    return jnp.concatenate([(d >= 0) & (d < meta[2]) for d in distances], 0)


def groups_of(heads):
    group = 2 if heads % 2 == 0 else 1
    wide = group * STRIPE
    return group, [pl.ds(i * wide, wide) for i in range(heads // group)]


def masked_scores(meta, q_ref, kv, turn, cols, group):
    scores = dot(rows_at(meta, kv, turn, 0), q_ref[cols], 1, 1)
    visible = jnp.concatenate([visible_at(meta, turn)] * group, 1)
    return jnp.where(visible, scores, neg_big)


def by_eight(value):
    return value.reshape(-1, 8, value.shape[1])


def find_weights(heads, keep, to_log2, meta, q_ref, kv, probs, run_max, run_sum, top, inverse):
    group, groups = groups_of(heads)
    turns, window_len = meta[1], meta[2]
    run_max[...] = jnp.full_like(run_max, neg_big)
    run_sum[...] = jnp.zeros_like(run_sum)

    def find_max(turn, masked):
        key_rows = rows_at(meta, kv, turn, 0)
        if masked:
            visible = jnp.concatenate([visible_at(meta, turn)] * group, 1)
        for cols in groups:
            scores = dot(key_rows, q_ref[cols], 1, 1)
            if masked:
                scores = jnp.where(visible, scores, neg_big)
            run_max[:, cols] = jnp.maximum(run_max[:, cols], jnp.max(by_eight(scores), axis=0))
            if keep:
                probs[turn, :, cols] = scores

    def add_max(turn, carry):
        _, backs = blocks_of(meta, turn)
        nearest, farthest = jnp.minimum(*backs), jnp.maximum(*backs)
        whole = (nearest >= 1) & (farthest * STRIPE + (STRIPE - 1) < window_len)

        @pl.when(whole)
        def _():
            find_max(turn, False)

        @pl.when(jnp.logical_not(whole))
        def _():
            find_max(turn, True)

        return carry

    lax.fori_loop(0, turns, add_max, 0)
    top[...] = jnp.max(run_max[...], axis=0, keepdims=True) * to_log2

    def add_sums(turn, carry):
        for cols in groups:
            if keep:
                scores = probs[turn, :, cols]
            else:
                scores = masked_scores(meta, q_ref, kv, turn, cols, group)
            part = jnp.exp2(scores * to_log2 - top[:, cols])
            run_sum[:, cols] += jnp.sum(by_eight(part), axis=0)
            if keep:
                probs[turn, :, cols] = part
        return carry

    lax.fori_loop(0, turns, add_sums, 0)
    inverse[...] = 1.0 / jnp.sum(run_sum[...], axis=0, keepdims=True)


def add_gradients(
    heads, keep, inv_scale, meta, begin, end,
    q_ref, g_ref, delta_ref, kv, probs, top, inverse, dq_ref, outs, buffers,
):
    group, groups = groups_of(heads)
    to_log2 = inv_scale * math.log2(math.e)

    def find_grads(turn, weight_buf, grad_buf):
        value_rows = rows_at(meta, kv, turn, STRIPE)
        for cols in groups:
            if keep:
                part = probs[turn, :, cols]
            else:
                scores = masked_scores(meta, q_ref, kv, turn, cols, group)
                part = jnp.exp2(scores * to_log2 - top[:, cols])
            weights = part * inverse[:, cols]
            weight_grad = dot(value_rows, g_ref[cols], 1, 1)
            score_grad = weights * (weight_grad - delta_ref[:, cols])
            weight_buf[:, cols] = weights.astype(jnp.bfloat16)
            grad_buf[:, cols] = score_grad.astype(jnp.bfloat16)

    def products(turn, weight_buf, grad_buf):
        score_grads = grad_buf[...]
        dq_ref[...] += dot(rows_at(meta, kv, turn, 0), score_grads, 0, 0)
        key_part = (dot(score_grads, q_ref[...], 1, 0) * inv_scale).astype(jnp.bfloat16)
        value_part = dot(weight_buf[...], g_ref[...], 1, 0).astype(jnp.bfloat16)
        return key_part, value_part

    def store(turn, parts):
        slots, _ = blocks_of(meta, turn)
        for i, slot in enumerate(slots):
            rows = slice(i * STRIPE, (i + 1) * STRIPE)
            for start, ref in outs:

                @pl.when((slot >= start) & (slot < start + ref.shape[0] // PAIR))
                def _(start=start, ref=ref):
                    inner = pl.multiple_of((slot - start) * PAIR, PAIR)
                    for j, part in enumerate(parts):
                        ref[pl.ds(inner + j * STRIPE, STRIPE)] = part[rows]

    for _, ref in outs:
        ref[...] = jnp.zeros_like(ref)
    weight_a, weight_b, grad_a, grad_b = buffers
    a, b = (weight_a, grad_a), (weight_b, grad_b)
    last = end - 1
    pairs = jnp.maximum(last - begin, 0) // 2

    def step(turn, now, before):
        parts = products(turn - 1, *before)
        find_grads(turn, *now)
        store(turn - 1, parts)

    def two_steps(pair, carry):
        turn = begin + 2 * pair
        step(turn + 1, b, a)
        step(turn + 2, a, b)
        return carry

    @pl.when(end > begin)
    def _():
        find_grads(begin, *a)
        lax.fori_loop(0, pairs, two_steps, 0)

    @pl.when((end > begin) & ((end - begin) % 2 == 0))
    def _():
        step(last, b, a)
        store(last, products(last, *b))

    @pl.when((end > begin) & ((end - begin) % 2 == 1))
    def _():
        store(last, products(last, *a))


def spans_of(stripes, pieces, refs, first_piece):
    length = stripes // 2 // pieces
    half = len(refs) // 2
    own = [((first_piece + i) * length, ref) for i, ref in enumerate(refs[:half])]
    other = [
        (stripes // 2 + (first_piece + i) * length, ref) for i, ref in enumerate(refs[half:])
    ]
    return own + other


def attend_early(stripes, pieces, heads, keep, inv_scale, meta, q_ref, g_ref, delta_ref, *refs):
    held, rest = refs[: 2 * pieces], refs[2 * pieces :]
    kv, probs, top, inverse, dq_ref, rest = *rest[:5], rest[5:]
    outs, rest = rest[:pieces], rest[pieces:]
    run_max, run_sum, *buffers = rest
    rows = held[0].shape[0]
    for i, piece in enumerate(held):
        kv[pl.ds(i * rows, rows)] = piece[...]
    kv[pl.ds(len(held) * rows, PAIR)] = jnp.zeros((PAIR, STRIPE), kv.dtype)
    dq_ref[...] = jnp.zeros_like(dq_ref)
    to_log2 = inv_scale * math.log2(math.e)
    find_weights(heads, keep, to_log2, meta, q_ref, kv, probs, run_max, run_sum, top, inverse)
    add_gradients(
        heads, keep, inv_scale, meta, 0, meta[0],
        q_ref, g_ref, delta_ref, kv, probs, top, inverse, dq_ref,
        spans_of(stripes, pieces, outs, pieces // 2), buffers,
    )


def attend_late(
    stripes, pieces, heads, keep, inv_scale,
    meta, q_ref, g_ref, delta_ref, kv, probs, top, inverse, dq_early, dq_ref, *refs,
):
    outs, buffers = refs[:pieces], refs[pieces:]
    dq_ref[...] = dq_early[...]
    add_gradients(
        heads, keep, inv_scale, meta, meta[0], meta[1],
        q_ref, g_ref, delta_ref, kv, probs, top, inverse, dq_ref,
        spans_of(stripes, pieces, outs, 0), buffers,
    )


def turn_queries(heads, inv_scale, turned, out):
    for head in range(heads):
        cols = pl.ds(head * STRIPE, STRIPE)
        out[:, cols] = (turned[:, cols].T * inv_scale).astype(jnp.bfloat16)


def vmem_limit(nbytes):
    return pltpu.CompilerParams(vmem_limit_bytes=nbytes)


vmem_spec = pl.BlockSpec(memory_space=pltpu.VMEM)
smem_spec = pl.BlockSpec(memory_space=pltpu.SMEM)


def run_prepare(layout, heads, here, order, window, queries, exps, grads, outs):
    flat = jax.ShapeDtypeStruct((heads * STRIPE, STRIPE), jnp.bfloat16)
    return pl.pallas_call(
        functools.partial(prepare, layout, heads),
        out_shape=[
            flat,
            flat,
            jax.ShapeDtypeStruct((1, heads * STRIPE), jnp.float32),
            jax.ShapeDtypeStruct((head_len + 2 * (layout.count + 2),), jnp.int32),
        ],
        in_specs=[smem_spec] * 3 + [vmem_spec] * 4,
        out_specs=[vmem_spec] * 3 + [smem_spec],
        compiler_params=vmem_limit(24 * STRIPE * heads * STRIPE * 2),
        name="prep",
    )(here, order, window, queries, exps, grads, outs)


def run_attend(early, meta, q_flat, g_flat, delta, others, pieces, stripes, heads, inv_scale):
    wide = q_flat.shape[0]
    turns = stripes // 2 + 2
    keep = turns * PAIR * wide * 4 <= keep_bytes
    half_rows = stripes // 2 * PAIR
    query_sum = jax.ShapeDtypeStruct((STRIPE, wide), jnp.float32)
    row = jax.ShapeDtypeStruct((1, wide), jnp.float32)
    outs = [query_sum] + [
        jax.ShapeDtypeStruct((half_rows // pieces, STRIPE), jnp.bfloat16)
    ] * pieces
    scratch = [pltpu.VMEM((PAIR, wide), jnp.bfloat16)] * 4
    if early:
        outs = [
            jax.ShapeDtypeStruct((2 * half_rows + PAIR, STRIPE), jnp.bfloat16),
            jax.ShapeDtypeStruct((turns if keep else 1, PAIR, wide), jnp.float32),
            row,
            row,
        ] + outs
        scratch = [pltpu.VMEM((8, wide), jnp.float32)] * 2 + scratch
    body = attend_early if early else attend_late
    return pl.pallas_call(
        functools.partial(body, stripes, pieces, heads, keep, inv_scale),
        out_shape=outs,
        in_specs=[smem_spec] + [vmem_spec] * (3 + len(others)),
        out_specs=[vmem_spec] * len(outs),
        scratch_shapes=scratch,
        compiler_params=vmem_limit(13 * half_rows * STRIPE + 12 * PAIR * wide * 2),
        name="early" if early else "late",
    )(meta, q_flat, g_flat, delta, *others)


def run_turn(turned, heads, inv_scale):
    return pl.pallas_call(
        functools.partial(turn_queries, heads, inv_scale),
        out_shape=jax.ShapeDtypeStruct(turned.shape, jnp.bfloat16),
        in_specs=[vmem_spec],
        out_specs=vmem_spec,
        compiler_params=vmem_limit(24 * STRIPE * heads * STRIPE * 2),
        name="turn",
    )(turned)


def per_device(
    layout,
    queries, query_exps, key_head, value_head, forward_out, output_grad, stripe_order, window_size
):
    head_dim = key_head.shape[1]
    tokens, feat_width = queries.shape
    heads = feat_width // head_dim
    inv_scale = 1.0 / math.sqrt(head_dim)
    stripes = layout.count
    row, col = lax.axis_index("row"), lax.axis_index("col")

    def send(value, **where):
        return lax.ppermute(value, AXES, layout.hop(**where))

    def widen(value):
        return value.astype(jnp.float32)

    pair = lax.optimization_barrier(jnp.concatenate([key_head, value_head], 0))
    stage = [pair] + [send(pair, first=i) for i in range(1, layout.near)]
    plane = jnp.concatenate(stage, 0)
    own_pieces = [plane] + [send(plane, second=j) for j in range(1, layout.far)]
    other_pieces = [send(piece, core_flip=1) for piece in own_pieces]

    here = jnp.stack([row, col]).astype(jnp.int32)
    q_flat, g_flat, delta, meta = run_prepare(
        layout, heads, here, stripe_order, window_size,
        queries, query_exps.reshape(1, -1), output_grad, forward_out,
    )
    pieces = layout.far
    split = pieces // 2
    results = run_attend(
        True, meta, q_flat, g_flat, delta, own_pieces + other_pieces,
        pieces, stripes, heads, inv_scale,
    )
    between, early_parts = results[:5], results[5:]
    results = run_attend(
        False, meta, q_flat, g_flat, delta, between, pieces, stripes, heads, inv_scale
    )
    turned, late_parts = results[0], results[1:]
    query_grad = run_turn(turned, heads, inv_scale)

    own_parts = late_parts[:split] + early_parts[:split]
    other_parts = late_parts[split:] + early_parts[split:]
    summed = [None] * pieces
    for j in reversed(range(pieces)):
        arrived = send(other_parts[j], core_flip=1)
        summed[j] = widen(own_parts[j]) + widen(arrived)
    plane_sum = summed[0]
    for j in range(1, pieces):
        plane_sum = plane_sum + widen(send(summed[j].astype(jnp.bfloat16), second=j))
    pair_sum = plane_sum[:PAIR]
    for i in range(1, layout.near):
        part = plane_sum[i * PAIR : (i + 1) * PAIR].astype(jnp.bfloat16)
        pair_sum = pair_sum + widen(send(part, first=i))
    pair_sum = pair_sum.astype(jnp.bfloat16)
    return (query_grad, pair_sum[:tokens], pair_sum[tokens:])


def solution(mesh):
    layout = Layout(mesh.shape["row"], mesh.shape["col"])

    def whole(*arrays):
        return per_device(layout, *arrays)

    return jax.shard_map(
        whole,
        mesh=mesh,
        in_specs=(
            P(("row", "col"), None),
            P(("row", "col")),
            P(("col", "row"), None),
            P(("col", "row"), None),
            P(("row", "col"), None),
            P(("row", "col"), None),
            P(),
            P(),
        ),
        out_specs=(P(("row", "col"), None), P(("col", "row"), None), P(("col", "row"), None)),
        check_vma=False,
    )
```

```python
import functools
import math

import jax
import jax.numpy as jnp
from jax import lax
from jax.experimental import pallas as pl
from jax.experimental.pallas import tpu as pltpu
from jax.sharding import PartitionSpec as P

STRIPE = 128
PAIR = 2 * STRIPE
AXES = ("row", "col")
neg_big = -1e30
far_blocks = 1 << 22
head_len = 3
keep_bytes = 24 << 20


class Layout:
    def __init__(self, rows, cols):
        self.rows, self.cols = rows, cols
        self.near, self.far = rows * 2, cols // 4
        self.square = self.near == self.far
        self.count = rows * cols

    def chip(self, row, col, kind):
        ring = col // 4
        half = ring // 2
        fold = half if kind == 0 else 0
        return row * 2 + (ring + fold) % 2, half * 2 + (col // 2) % 2

    def hop(self, first=0, second=0, core_flip=0):
        pairs = []
        for device in range(self.count):
            col = device % self.cols
            core = col % 2
            near, far = self.chip(device // self.cols, col, core)
            if self.square and core == 1:
                near, far = near ^ second, far ^ first
            else:
                near, far = near ^ first, far ^ second
            half = far // 2
            fold = half if core == 0 else 0
            col = (half * 2 + (near + fold) % 2) * 4 + (far % 2) * 2 + (core ^ core_flip)
            pairs.append((device, (near // 2) * self.cols + col))
        return pairs

    def slot(self, row, col, stored):
        core = (stored // self.rows) % 2
        places = []
        for kind in range(2):
            own = self.chip(row, col, kind)
            other = self.chip(stored % self.rows, stored // self.rows, kind)
            near, far = own[0] ^ other[0], own[1] ^ other[1]
            turned = self.square and kind == 1
            places.append(near * self.far + far if turned else far * self.near + near)
        place = jnp.where(core == 1, places[1], places[0])
        return place + jnp.where(core == col % 2, 0, self.count // 2)

    def early(self, slot):
        return slot % (self.count // 2) >= self.count // 4


def dot(left, right, left_dim, right_dim):
    return lax.dot_general(
        left, right, (((left_dim,), (right_dim,)), ((), ())), preferred_element_type=jnp.float32
    )


def prepare(
    layout, heads, here, order, window, q_ref, e_ref, g_ref, o_ref, q_out, g_out, d_out, meta
):
    row, col = here[0], here[1]
    own_block = order[row * layout.cols + col]
    live = jnp.minimum(own_block, (window[0] + STRIPE - 2) // STRIPE) + 1
    part_len = layout.count + 2

    def write(part, place, slot, back):
        start = head_len + part * part_len + 2 * place
        meta[start] = slot
        meta[start + 1] = back

    def visit(stored, filled):
        back = own_block - order[stored]
        slot = layout.slot(row, col, stored)
        early = layout.early(slot)
        wanted = (back >= 0) & (back < live)

        @pl.when(wanted)
        def _():
            write(jnp.where(early, 0, 1), jnp.where(early, filled[0], filled[1]), slot, back)

        return (
            filled[0] + (wanted & early).astype(jnp.int32),
            filled[1] + (wanted & jnp.logical_not(early)).astype(jnp.int32),
        )

    filled = lax.fori_loop(0, layout.count, visit, (jnp.int32(0), jnp.int32(0)))
    turns = [(count + 1) // 2 for count in filled]
    for part, count in enumerate(filled):
        write(part, count, layout.count, far_blocks)
    meta[0] = turns[0]
    meta[1] = turns[0] + turns[1]
    meta[2] = window[0]
    power = jnp.left_shift(1, e_ref[...] + 1).astype(jnp.float32) * 0.5
    power = jnp.broadcast_to(power, (STRIPE, STRIPE)).T
    for head in range(heads):
        cols = pl.ds(head * STRIPE, STRIPE)
        q_out[cols] = (q_ref[:, cols].astype(jnp.float32) * power).astype(jnp.bfloat16)
        grads = g_ref[:, cols]
        g_out[cols] = grads
        product = grads.astype(jnp.float32) * o_ref[:, cols].astype(jnp.float32)
        sums = jnp.sum(product.T, axis=0, keepdims=True)
        d_out[:, cols] = sums.astype(jnp.bfloat16).astype(jnp.float32)


def blocks_of(meta, turn):
    part_len = (meta.shape[0] - head_len) // 2
    early = meta[0]
    start = head_len + jnp.where(turn < early, 4 * turn, part_len + 4 * (turn - early))
    return [meta[start], meta[start + 2]], [meta[start + 1], meta[start + 3]]


def rows_at(meta, kv, turn, shift):
    slots, _ = blocks_of(meta, turn)
    return jnp.concatenate(
        [kv[pl.ds(pl.multiple_of(slot * PAIR, PAIR) + shift, STRIPE)] for slot in slots], 0
    )


def visible_at(meta, turn):
    relative = lax.broadcasted_iota(jnp.int32, (STRIPE, STRIPE), 1) - lax.broadcasted_iota(
        jnp.int32, (STRIPE, STRIPE), 0
    )
    _, backs = blocks_of(meta, turn)
    distances = [relative + back * STRIPE for back in backs]
    return jnp.concatenate([(d >= 0) & (d < meta[2]) for d in distances], 0)


def groups_of(heads):
    group = 4 if heads % 4 == 0 else 1
    wide = group * STRIPE
    return group, [pl.ds(i * wide, wide) for i in range(heads // group)]


def masked_scores(meta, q_ref, kv, turn, cols, group):
    scores = dot(rows_at(meta, kv, turn, 0), q_ref[cols], 1, 1)
    visible = jnp.concatenate([visible_at(meta, turn)] * group, 1)
    return jnp.where(visible, scores, neg_big)


def by_eight(value):
    return value.reshape(-1, 8, value.shape[1])


def find_weights(heads, keep, to_log2, meta, q_ref, kv, probs, run_max, run_sum, top, inverse):
    group, groups = groups_of(heads)
    turns, window_len = meta[1], meta[2]
    run_max[...] = jnp.full_like(run_max, neg_big)
    run_sum[...] = jnp.zeros_like(run_sum)

    def find_max(turn, masked):
        key_rows = rows_at(meta, kv, turn, 0)
        if masked:
            visible = jnp.concatenate([visible_at(meta, turn)] * group, 1)
        for cols in groups:
            scores = dot(key_rows, q_ref[cols], 1, 1)
            if masked:
                scores = jnp.where(visible, scores, neg_big)
            run_max[:, cols] = jnp.maximum(run_max[:, cols], jnp.max(by_eight(scores), axis=0))
            if keep:
                probs[turn, :, cols] = scores

    def add_max(turn, carry):
        _, backs = blocks_of(meta, turn)
        nearest, farthest = jnp.minimum(*backs), jnp.maximum(*backs)
        whole = (nearest >= 1) & (farthest * STRIPE + (STRIPE - 1) < window_len)

        @pl.when(whole)
        def _():
            find_max(turn, False)

        @pl.when(jnp.logical_not(whole))
        def _():
            find_max(turn, True)

        return carry

    lax.fori_loop(0, turns, add_max, 0)
    top[...] = jnp.max(run_max[...], axis=0, keepdims=True) * to_log2

    def add_sums(turn, carry):
        for cols in groups:
            if keep:
                scores = probs[turn, :, cols]
            else:
                scores = masked_scores(meta, q_ref, kv, turn, cols, group)
            part = jnp.exp2(scores * to_log2 - top[:, cols])
            run_sum[:, cols] += jnp.sum(by_eight(part), axis=0)
            if keep:
                probs[turn, :, cols] = part
        return carry

    lax.fori_loop(0, turns, add_sums, 0)
    inverse[...] = 1.0 / jnp.sum(run_sum[...], axis=0, keepdims=True)


def add_gradients(
    heads, keep, inv_scale, meta, begin, end,
    q_ref, g_ref, delta_ref, kv, probs, top, inverse, dq_ref, outs, buffers,
):
    group, groups = groups_of(heads)
    to_log2 = inv_scale * math.log2(math.e)

    def find_grads(turn, weight_buf, grad_buf):
        value_rows = rows_at(meta, kv, turn, STRIPE)
        for cols in groups:
            if keep:
                part = probs[turn, :, cols]
            else:
                scores = masked_scores(meta, q_ref, kv, turn, cols, group)
                part = jnp.exp2(scores * to_log2 - top[:, cols])
            weights = part * inverse[:, cols]
            weight_grad = dot(value_rows, g_ref[cols], 1, 1)
            score_grad = weights * (weight_grad - delta_ref[:, cols])
            weight_buf[:, cols] = weights.astype(jnp.bfloat16)
            grad_buf[:, cols] = score_grad.astype(jnp.bfloat16)

    def products(turn, weight_buf, grad_buf):
        score_grads = grad_buf[...]
        dq_ref[...] += dot(rows_at(meta, kv, turn, 0), score_grads, 0, 0)
        key_part = (dot(score_grads, q_ref[...], 1, 0) * inv_scale).astype(jnp.bfloat16)
        value_part = dot(weight_buf[...], g_ref[...], 1, 0).astype(jnp.bfloat16)
        return key_part, value_part

    def store(turn, parts):
        slots, _ = blocks_of(meta, turn)
        for i, slot in enumerate(slots):
            rows = slice(i * STRIPE, (i + 1) * STRIPE)
            for start, ref in outs:

                @pl.when((slot >= start) & (slot < start + ref.shape[0] // PAIR))
                def _(start=start, ref=ref):
                    inner = pl.multiple_of((slot - start) * PAIR, PAIR)
                    for j, part in enumerate(parts):
                        ref[pl.ds(inner + j * STRIPE, STRIPE)] = part[rows]

    for _, ref in outs:
        ref[...] = jnp.zeros_like(ref)
    weight_a, weight_b, grad_a, grad_b = buffers
    a, b = (weight_a, grad_a), (weight_b, grad_b)
    last = end - 1
    pairs = jnp.maximum(last - begin, 0) // 2

    def step(turn, now, before):
        parts = products(turn - 1, *before)
        find_grads(turn, *now)
        store(turn - 1, parts)

    def two_steps(pair, carry):
        turn = begin + 2 * pair
        step(turn + 1, b, a)
        step(turn + 2, a, b)
        return carry

    @pl.when(end > begin)
    def _():
        find_grads(begin, *a)
        lax.fori_loop(0, pairs, two_steps, 0)

    @pl.when((end > begin) & ((end - begin) % 2 == 0))
    def _():
        step(last, b, a)
        store(last, products(last, *b))

    @pl.when((end > begin) & ((end - begin) % 2 == 1))
    def _():
        store(last, products(last, *a))


def spans_of(stripes, pieces, refs, first_piece):
    length = stripes // 2 // pieces
    half = len(refs) // 2
    own = [((first_piece + i) * length, ref) for i, ref in enumerate(refs[:half])]
    other = [
        (stripes // 2 + (first_piece + i) * length, ref) for i, ref in enumerate(refs[half:])
    ]
    return own + other


def attend_early(stripes, pieces, heads, keep, inv_scale, meta, q_ref, g_ref, delta_ref, *refs):
    held, rest = refs[: 2 * pieces], refs[2 * pieces :]
    kv, probs, top, inverse, dq_ref, rest = *rest[:5], rest[5:]
    outs, rest = rest[:pieces], rest[pieces:]
    run_max, run_sum, *buffers = rest
    rows = held[0].shape[0]
    for i, piece in enumerate(held):
        kv[pl.ds(i * rows, rows)] = piece[...]
    kv[pl.ds(len(held) * rows, PAIR)] = jnp.zeros((PAIR, STRIPE), kv.dtype)
    dq_ref[...] = jnp.zeros_like(dq_ref)
    to_log2 = inv_scale * math.log2(math.e)
    find_weights(heads, keep, to_log2, meta, q_ref, kv, probs, run_max, run_sum, top, inverse)
    add_gradients(
        heads, keep, inv_scale, meta, 0, meta[0],
        q_ref, g_ref, delta_ref, kv, probs, top, inverse, dq_ref,
        spans_of(stripes, pieces, outs, pieces // 2), buffers,
    )


def attend_late(
    stripes, pieces, heads, keep, inv_scale,
    meta, q_ref, g_ref, delta_ref, kv, probs, top, inverse, dq_early, dq_ref, *refs,
):
    outs, buffers = refs[:pieces], refs[pieces:]
    dq_ref[...] = dq_early[...]
    add_gradients(
        heads, keep, inv_scale, meta, meta[0], meta[1],
        q_ref, g_ref, delta_ref, kv, probs, top, inverse, dq_ref,
        spans_of(stripes, pieces, outs, 0), buffers,
    )


def turn_queries(heads, inv_scale, turned, out):
    for head in range(heads):
        cols = pl.ds(head * STRIPE, STRIPE)
        out[:, cols] = (turned[:, cols].T * inv_scale).astype(jnp.bfloat16)


def vmem_limit(nbytes):
    return pltpu.CompilerParams(vmem_limit_bytes=nbytes)


vmem_spec = pl.BlockSpec(memory_space=pltpu.VMEM)
smem_spec = pl.BlockSpec(memory_space=pltpu.SMEM)


def run_prepare(layout, heads, here, order, window, queries, exps, grads, outs):
    flat = jax.ShapeDtypeStruct((heads * STRIPE, STRIPE), jnp.bfloat16)
    return pl.pallas_call(
        functools.partial(prepare, layout, heads),
        out_shape=[
            flat,
            flat,
            jax.ShapeDtypeStruct((1, heads * STRIPE), jnp.float32),
            jax.ShapeDtypeStruct((head_len + 2 * (layout.count + 2),), jnp.int32),
        ],
        in_specs=[smem_spec] * 3 + [vmem_spec] * 4,
        out_specs=[vmem_spec] * 3 + [smem_spec],
        compiler_params=vmem_limit(24 * STRIPE * heads * STRIPE * 2),
        name="prep",
    )(here, order, window, queries, exps, grads, outs)


def run_attend(early, meta, q_flat, g_flat, delta, others, pieces, stripes, heads, inv_scale):
    wide = q_flat.shape[0]
    turns = stripes // 2 + 2
    keep = turns * PAIR * wide * 4 <= keep_bytes
    half_rows = stripes // 2 * PAIR
    query_sum = jax.ShapeDtypeStruct((STRIPE, wide), jnp.float32)
    row = jax.ShapeDtypeStruct((1, wide), jnp.float32)
    outs = [query_sum] + [
        jax.ShapeDtypeStruct((half_rows // pieces, STRIPE), jnp.bfloat16)
    ] * pieces
    scratch = [pltpu.VMEM((PAIR, wide), jnp.bfloat16)] * 4
    if early:
        outs = [
            jax.ShapeDtypeStruct((2 * half_rows + PAIR, STRIPE), jnp.bfloat16),
            jax.ShapeDtypeStruct((turns if keep else 1, PAIR, wide), jnp.float32),
            row,
            row,
        ] + outs
        scratch = [pltpu.VMEM((8, wide), jnp.float32)] * 2 + scratch
    body = attend_early if early else attend_late
    return pl.pallas_call(
        functools.partial(body, stripes, pieces, heads, keep, inv_scale),
        out_shape=outs,
        in_specs=[smem_spec] + [vmem_spec] * (3 + len(others)),
        out_specs=[vmem_spec] * len(outs),
        scratch_shapes=scratch,
        compiler_params=pltpu.CompilerParams(
            vmem_limit_bytes=13 * half_rows * STRIPE + 12 * PAIR * wide * 2,
        ),
        name="early" if early else "late",
    )(meta, q_flat, g_flat, delta, *others)


def run_turn(turned, heads, inv_scale):
    return pl.pallas_call(
        functools.partial(turn_queries, heads, inv_scale),
        out_shape=jax.ShapeDtypeStruct(turned.shape, jnp.bfloat16),
        in_specs=[vmem_spec],
        out_specs=vmem_spec,
        compiler_params=vmem_limit(24 * STRIPE * heads * STRIPE * 2),
        name="turn",
    )(turned)


def per_device(
    layout,
    queries, query_exps, key_head, value_head, forward_out, output_grad, stripe_order, window_size
):
    head_dim = key_head.shape[1]
    tokens, feat_width = queries.shape
    heads = feat_width // head_dim
    inv_scale = 1.0 / math.sqrt(head_dim)
    stripes = layout.count
    row, col = lax.axis_index("row"), lax.axis_index("col")

    def send(value, **where):
        return lax.ppermute(value, AXES, layout.hop(**where))

    def widen(value):
        return value.astype(jnp.float32)

    pair = lax.optimization_barrier(jnp.concatenate([key_head, value_head], 0))
    stage = [pair] + [send(pair, first=i) for i in range(1, layout.near)]
    plane = jnp.concatenate(stage, 0)
    own_pieces = [plane] + [send(plane, second=j) for j in range(1, layout.far)]
    other_pieces = [send(piece, core_flip=1) for piece in own_pieces]

    here = jnp.stack([row, col]).astype(jnp.int32)
    q_flat, g_flat, delta, meta = run_prepare(
        layout, heads, here, stripe_order, window_size,
        queries, query_exps.reshape(1, -1), output_grad, forward_out,
    )
    pieces = layout.far
    split = pieces // 2
    results = run_attend(
        True, meta, q_flat, g_flat, delta, own_pieces + other_pieces,
        pieces, stripes, heads, inv_scale,
    )
    between, early_parts = results[:5], results[5:]
    results = run_attend(
        False, meta, q_flat, g_flat, delta, between, pieces, stripes, heads, inv_scale
    )
    turned, late_parts = results[0], results[1:]
    query_grad = run_turn(turned, heads, inv_scale)

    own_parts = late_parts[:split] + early_parts[:split]
    other_parts = late_parts[split:] + early_parts[split:]
    summed = [None] * pieces
    for j in reversed(range(pieces)):
        arrived = send(other_parts[j], core_flip=1)
        summed[j] = widen(own_parts[j]) + widen(arrived)
    plane_sum = summed[0]
    for j in range(1, pieces):
        plane_sum = plane_sum + widen(send(summed[j].astype(jnp.bfloat16), second=j))
    pair_sum = plane_sum[:PAIR]
    for i in range(1, layout.near):
        part = plane_sum[i * PAIR : (i + 1) * PAIR].astype(jnp.bfloat16)
        pair_sum = pair_sum + widen(send(part, first=i))
    pair_sum = pair_sum.astype(jnp.bfloat16)
    return (query_grad, pair_sum[:tokens], pair_sum[tokens:])


def solution(mesh):
    layout = Layout(mesh.shape["row"], mesh.shape["col"])

    def whole(*arrays):
        return per_device(layout, *arrays)

    return jax.shard_map(
        whole,
        mesh=mesh,
        in_specs=(
            P(("row", "col"), None),
            P(("row", "col")),
            P(("col", "row"), None),
            P(("col", "row"), None),
            P(("row", "col"), None),
            P(("row", "col"), None),
            P(),
            P(),
        ),
        out_specs=(P(("row", "col"), None), P(("col", "row"), None), P(("col", "row"), None)),
        check_vma=False,
    )
```
